32 devices in a mesh: row: 16 (over z, x, core), col: 2 (over y).
Axes of the slice: x: 2, y: 2, z: 4, core: 2. Of those that a mesh axis runs over, the one named last changes fastest.
Arguments:
- embeddings: bfloat16 [16384, 768], P(('row', 'col')), may hold values from -7.5 to 7.5
- block_cluster: int32 [64], replicated, may hold values from 0 to 15, never falling along the last dimension, each value on 1 to 8 neighbouring positions
- partner_shift: int32 [16384], P(('row', 'col')), may hold values from 1 to 255
Outputs:
- item_loss: float32 [16384], P(('row', 'col'))
- embedding_grad: float32 [16384, 768], P(('row', 'col'))
The draws below stay inside these ranges and needn't reach their ends.
Inputs may be any that keep to these rules, and one draw needn't show every extreme that they name: block_cluster never falls along the blocks; each value is held by 1 to 8 consecutive blocks, and some value by exactly 8.
All inputs are finite; a program needn't handle non-finite values.
Results may differ from the reference program's by a relative error of at most 0.0018.
Values may be sent and summed in bfloat16 or wider, within the bound.
A program may use at most 128 MiB of HBM per device.

```python
import math
import jax
import jax.numpy as jnp
import numpy as np
from jax import lax

D = 768
BLOCK = 256
MOST = 8
ITEMS = 16384
BLOCKS = 64
CLUSTERS = 16


def draw_embeddings(key, part):
    k_base, k_scale = jax.random.split(key, 2)
    base = jax.random.normal(k_base, (ITEMS, D), jnp.float32)
    spread = jax.random.uniform(k_scale, (ITEMS, 1), jnp.float32, math.log(0.5), math.log(2.0))
    values = jnp.clip(base * jnp.exp(spread), -7.5, 7.5)
    return values.astype(jnp.bfloat16)


def plant(entries, own_key, least, high):
    longest = entries.shape.index(max(entries.shape))
    spots = []
    for shift in (0, 1):
        where = [jax.random.randint(jax.random.fold_in(own_key, axis), (), 0, length) for axis, length in enumerate(entries.shape)]
        where[longest] = (where[longest] + shift) % entries.shape[longest]
        spots.append(tuple(where))
    return entries.at[spots[0]].set(least).at[spots[1]].set(high)


def length_profile(number_of, total, limit, lean):
    loads = [(1 << 20) // math.isqrt(standing ** lean) + 1 for standing in range(2, number_of + 1)]
    rest, given = total - limit - (number_of - 1), [1] * (number_of - 1)
    while rest > 0:
        movable = [i for i in range(number_of - 1) if given[i] < limit]
        whole, remaining = sum([loads[i] for i in movable]), rest
        for i in movable:
            extra = min(limit - given[i], max(1, remaining * loads[i] // whole), rest)
            given[i] = given[i] + extra
            rest = rest - extra
    return np.array([limit] + given)


def uneven_parts(stream_key, number_of, total, most, slope):
    if number_of == 2:
        one = jax.random.randint(stream_key, (), max(1, total - most), min(most, total - 1) + 1)
        return jnp.stack([one, total - one])
    sizes = jnp.asarray(length_profile(number_of, total, most, slope), jnp.int32)
    couples = (number_of - 1) // 2
    giver, taker = sizes[1:1 + 2 * couples:2], sizes[2:2 + 2 * couples:2]
    room = jnp.minimum(giver - 1, most - taker)
    moved = jax.random.randint(jax.random.fold_in(stream_key, 1), (couples,), 0, 1 << 20) % (room + 1)
    sizes = sizes.at[1:1 + 2 * couples:2].set(giver - moved).at[2:2 + 2 * couples:2].set(taker + moved)
    return sizes[jax.random.permutation(jax.random.fold_in(stream_key, 2), number_of)]


def setup_inputs(seed: int = 0) -> dict:
    key_list = jax.random.split(jax.random.key(seed), 4)
    embeddings = draw_embeddings(jax.random.fold_in(key_list[3], 71), 0)
    block_cluster = jnp.searchsorted(jnp.cumsum(uneven_parts(key_list[1], CLUSTERS, BLOCKS, MOST, 2)), jnp.arange(BLOCKS), side="right").astype(jnp.int32)
    partner_shift = plant(jax.random.randint(key_list[2], (ITEMS,), 1, BLOCK), jax.random.fold_in(key_list[2], 1), 1, BLOCK - 1).astype(jnp.int32)
    return {"embeddings": embeddings, "block_cluster": block_cluster, "partner_shift": partner_shift}


NEG = -1.0e30


def shift_blocks(values, offset):
    if offset == 0:
        return values
    pad = jnp.zeros((abs(offset),) + values.shape[1:], values.dtype)
    if offset > 0:
        return jnp.concatenate([values[offset:], pad], 0)
    return jnp.concatenate([pad, values[:offset]], 0)


def reference(embeddings, block_cluster, partner_shift):
    nblocks = ITEMS // BLOCK
    scale = D ** -0.5
    span = MOST - 1
    blocked = embeddings.astype(jnp.float32).reshape(nblocks, BLOCK, D)
    index = jnp.arange(nblocks, dtype=jnp.int32)
    position = jnp.arange(BLOCK, dtype=jnp.int32)
    diagonal = position[:, None] == position[None, :]

    def live_at(offset):
        valid = (index + offset >= 0) & (index + offset < nblocks)
        same = block_cluster == shift_blocks(block_cluster, offset)
        live = jnp.broadcast_to((valid & same)[:, None, None], (nblocks, BLOCK, BLOCK))
        if offset == 0:
            live = live & jnp.logical_not(diagonal)[None]
        return live

    def scores_at(offset):
        partner = shift_blocks(blocked, offset)
        return jnp.einsum("abd,acd->abc", blocked, partner, precision=lax.Precision.HIGHEST) * scale

    top = jnp.full((nblocks, BLOCK), NEG, jnp.float32)
    total = jnp.zeros((nblocks, BLOCK), jnp.float32)
    for offset in range(-span, span + 1):
        live = live_at(offset)
        masked = jnp.where(live, scores_at(offset), NEG)
        new_top = jnp.maximum(top, jnp.max(masked, axis=2))
        total = total * jnp.exp(top - new_top) + jnp.sum(jnp.where(live, jnp.exp(masked - new_top[:, :, None]), 0.0), axis=2)
        top = new_top
    lse = top + jnp.log(total)

    shifts = partner_shift.reshape(nblocks, BLOCK)
    partner = (position[None, :] + shifts) % BLOCK
    positive = position[None, None, :] == partner[:, :, None]
    self_scores = scores_at(0)
    loss = lse - jnp.sum(jnp.where(positive, self_scores, 0.0), axis=2)

    grad = jnp.zeros((nblocks, BLOCK, D), jnp.float32)
    for offset in range(-span, span + 1):
        live = live_at(offset)
        scores = scores_at(offset)
        rowwise = jnp.exp(jnp.where(live, scores - lse[:, :, None], NEG))
        if offset == 0:
            rowwise = rowwise - positive.astype(jnp.float32)
            both = rowwise + jnp.swapaxes(rowwise, 1, 2)
        else:
            far = shift_blocks(lse, offset)
            both = rowwise + jnp.exp(jnp.where(live, scores - far[:, None, :], NEG))
        weights = lax.optimization_barrier(both.astype(jnp.bfloat16)).astype(jnp.float32)
        grad = grad + jnp.einsum("abc,acd->abd", weights, shift_blocks(blocked, offset), precision=lax.Precision.HIGHEST) * scale
    return loss.reshape(ITEMS), grad.reshape(ITEMS, D)
```

```python
import functools

import jax
import jax.numpy as jnp
from jax import lax
from jax.experimental import pallas as pl
from jax.experimental.pallas import tpu as pltpu
from jax.sharding import PartitionSpec as P

BLOCK = 256
MOST = 8
REACH = 4
CHUNK = 128
HALF = 64
NEG = -1e30
F32 = jnp.float32
MESH = pl.DeviceIdType.MESH

X_IN = (
    (40, 41, 34, 35, 36, 37, 38, 39, 32, 33, 10, 11),
    (38, 44, 39, 45, 43, 42, 14, 15, 33, 32, 37, 36),
)
Y_IN = (
    (20, 21, 30, 31, 22, 23, 28, 29, 12, 13, 14, 15),
    (27, 26, 25, 24, 40, 41, 16, 17, 18, 19, 34, 35),
)
Z_IN = (
    (8, 9, 2, 3, 4, 5, 6, 7),
    (6, 12, 7, 13, 8, 11, 9, 10),
)
BACK = ((17, 16), (21, 20))
OWN = (((16, 17, 18, 19), (24, 25, 26, 27)), ((20, 21, 22, 23), (28, 29, 30, 31)))
SCORE = (
    (
        {0: (12, 13), 2: (10,), 4: (4, 15), 6: (1, 11), 8: (2, 14), 10: (3, 16), 11: (6,), 12: (5, 7)},
        {0: (8, 9), 2: (20, 10), 4: (17, 15), 6: (18, 11), 8: (19, 14), 10: (16, 6), 12: (5, 7)},
    ),
    (
        {0: (14, 15), 2: (13,), 4: (12,), 5: (3,), 6: (6,), 8: (7, 8), 9: (4,), 10: (5, 9), 11: (16,), 12: (17, 18)},
        {0: (10, 11), 2: (13,), 3: (19,), 4: (12, 22), 6: (20, 21), 8: (7, 8), 10: (9, 16), 12: (17, 18)},
    ),
)
STEPS = 13


def events_of(t):
    x_out = [("T", s - (14 if t == 0 else 10)) if s < 16 else ("S", 63 - s) for s in X_IN[1 - t]]
    y_out = [("S", s) for s in Y_IN[1 - t]]
    z_out = [("S", s + 32) for s in Z_IN[t]]
    lists = {"X": x_out, "Y": y_out, "Z": z_out}
    ahead = {"X": 0, "Y": 0, "Z": 0}
    have = {("S", s) for c in range(2) for s in OWN[t][c]}

    def ready():
        out = []
        for link, items in lists.items():
            while ahead[link] < len(items) and items[ahead[link]] in have:
                out.append((link, ahead[link]))
                ahead[link] += 1
        return out

    first = ready()
    steps = []
    for u in range(STEPS):
        now = []
        if u < 12:
            now += [("X", u, ("S", X_IN[t][u])), ("Y", u, ("S", Y_IN[t][u]))]
        if u < 2:
            now.append(("T", u, ("T", u)))
        if 2 <= u < 10:
            now.append(("Z", u - 2, ("S", Z_IN[t][u - 2])))
        done = []
        for kind, i, item in now:
            have.add(item)
            done.append((kind, i, ready()))
        steps.append(done)
    assert all(ahead[link] == len(items) for link, items in lists.items())
    return lists, first, steps


def kernel(
    row_axis, col_axis, devices, cols, scale,
    cluster_hbm, e_hbm, shift_hbm,
    grad_ref, loss_ref,
    buf, thru, scores, first_exp, weights, top, total, lse_col, lse_send, lse_far, pos_score, qcol_ref, qrow_ref,
    cluster_ref, shift_ref,
    recv, trecv, xs, ys, zs, bs, cs, ls, lr, own_sem,
):
    me = lax.axis_index(row_axis) * cols + lax.axis_index(col_axis)
    y = me % 2
    c = me // 2 % 2
    x = me // 4 % 2
    g = 2 * c + y
    yt = (x + y) % 2
    ct = (x + c) % 2
    xpeer = me + 4 - 8 * x
    ypeer = me + 1 - 2 * y
    cpeer = me + 2 - 4 * c
    zto = me + 8 - 16 * x
    zfrom = me - 8 + 16 * x
    z_send = (zto >= 0) & (zto < devices)
    z_recv = (zfrom >= 0) & (zfrom < devices)

    def at(device):
        return (device // cols, device % cols)

    def exists(device):
        return (device >= 0) & (device < devices)

    def when(cond, action):
        if cond is True:
            action()
        else:
            pl.when(cond)(action)

    def both(*conds):
        conds = [cond for cond in conds if cond is not True]
        return functools.reduce(lambda a, b: a & b, conds) if conds else True

    barrier = pltpu.get_barrier_semaphore()
    count = jnp.int32(0)
    for there, device in ((True, xpeer), (True, ypeer), (True, cpeer), (z_send, zto), (z_recv, zfrom)):
        when(there, lambda: pl.semaphore_signal(barrier, inc=1, device_id=at(device), device_id_type=MESH))
        count = count + (1 if there is True else there.astype(jnp.int32))
    pl.semaphore_wait(barrier, count)

    n = e_hbm.shape[0]
    first = 8 + 2 * g

    def slot_of(s):
        return s + x * (47 - 2 * s)

    def rows(slot, half):
        return buf.at[slot // 2, pl.ds(pl.multiple_of(slot % 2 * CHUNK + half * HALF, HALF), HALF), :]

    def copy(src, dst, send, receive, device):
        return pltpu.make_async_remote_copy(
            src_ref=src, dst_ref=dst, send_sem=send, recv_sem=receive,
            device_id=at(device), device_id_type=MESH,
        )

    def arrived(slot, half):
        copy(rows(slot, half), rows(slot, half), cs.at[0], recv.at[2 * slot + half], cpeer).wait_recv()

    def mine(s):
        return e_hbm.at[pl.ds(pl.multiple_of((slot_of(s) - 16 - 4 * g) * CHUNK + c * HALF, HALF), HALF), :]

    def source(t, item, own=False):
        kind, s = item
        if kind == "T":
            return thru.at[pl.ds(s * HALF, HALF), :]
        return mine(s) if own else rows(slot_of(s), c)

    def link_copy(t, lists, link, i, own=False):
        item = lists[link][i]
        src = source(t, item, own)
        if link == "X":
            s = X_IN[1 - t][i]
            slot = s + (1 - x) * (47 - 2 * s)
            return copy(src, rows(slot, c), xs.at[i], recv.at[2 * slot + c], xpeer)
        if link == "Y":
            slot = slot_of(Y_IN[1 - t][i])
            return copy(src, rows(slot, c), ys.at[i], recv.at[2 * slot + c], ypeer)
        slot = slot_of(Z_IN[t][i])
        return copy(src, rows(slot, c), zs.at[i], recv.at[2 * slot + c], zto)

    def link_cond(t, link, i):
        if link == "Z":
            return z_send
        if link == "X":
            return z_send if X_IN[1 - t][i] < 16 else True
        return z_recv if Y_IN[1 - t][i] < 16 else True

    def back_copy(t, i, own=False):
        src = source(t, ("S", BACK[t][i]), own)
        return copy(src, thru.at[pl.ds(i * HALF, HALF), :], bs.at[i], trecv.at[i], zfrom)

    def own_half(i, half):
        return e_hbm.at[pl.ds(i * CHUNK + half * HALF, HALF), :]

    def c_own(i, half, j):
        slot = 16 + 4 * g + i
        return copy(own_half(i, half), rows(slot, half), cs.at[32 + j], recv.at[2 * slot + half], cpeer)

    def c_copy(s, j):
        slot = slot_of(s)
        return copy(rows(slot, c), rows(slot, c), cs.at[j], recv.at[2 * slot + c], cpeer)

    def c_cond(t, s):
        low = [8 * k + 4 * t + 2 <= s <= 8 * k + 4 * t + 33 for k in range(2)]
        if low[0] and low[1]:
            need = True
        elif low[0]:
            need = ct == 1
        elif low[1]:
            need = ct == 0
        else:
            return False
        return both(need, z_recv if s < 16 else True)

    def c_all(t):
        places = [(s, j) for j, s in enumerate(X_IN[t] + Y_IN[t] + Z_IN[t])]
        return [(s, j, c_cond(t, s)) for s, j in places if c_cond(t, s) is not False]

    plans = [events_of(t) for t in range(2)]

    own_copies = [
        pltpu.make_async_copy(e_hbm.at[pl.ds(h * BLOCK, BLOCK), :], buf.at[first + h], own_sem.at[3 * h]) for h in range(2)]
    cluster_copy = pltpu.make_async_copy(cluster_hbm, cluster_ref, own_sem.at[1])
    shift_copy = pltpu.make_async_copy(shift_hbm, shift_ref, own_sem.at[2])
    for t in range(2):
        for k in range(2):
            @pl.when((yt == t) & (ct == k))
            def _():
                lists, first, _ = plans[t]
                opening = [(link, i) for link, i in first] + [("B", i) for i in range(2)]

                def slot_at(link, i):
                    return BACK[t][i] if link == "B" else lists[link][i][1]

                def send(link, i, own):
                    if link == "B":
                        when(z_recv, lambda: back_copy(t, i, own).start())
                    else:
                        when(link_cond(t, link, i), lambda: link_copy(t, lists, link, i, own).start())

                started = {"X": 0, "Y": 0, "B": 0}
                queue = {link: [i for name, i in opening if name == link] for link in ("X", "Y", "B")}
                plan = {}
                for link, items in queue.items():
                    mine_, other = ([i for i in items if (slot_at(link, i) in OWN[t][k]) == flag] for flag in (True, False))
                    order = []
                    for spot in range(len(items)):
                        take = mine_ if (spot == 0 and mine_) or not other or (mine_ and mine_[0] < other[0]) else other
                        order.append(take.pop(0))
                    plan[link] = order
                leads = []
                for link in ("Y", "X", "B"):
                    while plan[link] and slot_at(link, plan[link][0]) in OWN[t][k]:
                        leads.append((link, plan[link].pop(0)))
                for link, i in leads[:2]:
                    send(link, i, True)
                uses = []
                for link in ("Y", "X", "B", "Y", "X", "B", "Y", "X", "B", "Y", "X", "B", "Y", "Y", "Y", "Y", "X", "X"):
                    if plan[link]:
                        uses.append((link, plan[link].pop(0)))
                assert not any(plan.values())
                order = []
                for s in [s for link, i in [*leads, *uses] for s in [slot_at(link, i)]] + list(OWN[t][k]):
                    if s in OWN[t][k] and s not in order:
                        order.append(s)
                for j, s in enumerate(order):
                    i = slot_of(s) - 16 - 4 * g
                    copy(
                        e_hbm.at[pl.ds(pl.multiple_of(i * CHUNK + (1 - c) * HALF, HALF), HALF), :],
                        rows(slot_of(s), 1 - c), cs.at[32 + j], recv.at[2 * slot_of(s) + 1 - c], cpeer).start()
                for link, i in leads[2:]:
                    send(link, i, True)
                for own_copy in own_copies:
                    own_copy.start()
                cluster_copy.start()
                shift_copy.start()
                for j, s in enumerate(order):
                    copy(mine(s), rows(slot_of(s), c), cs.at[36 + j], recv.at[2 * slot_of(s) + c], cpeer).start()
                waited = set()
                for link, i in uses:
                    s = slot_at(link, i)
                    if s in OWN[t][k]:
                        send(link, i, True)
                        continue
                    if s not in waited:
                        waited.add(s)
                        arrived(slot_of(s), c)
                    send(link, i, False)
                for s in OWN[t][1 - k]:
                    if s not in waited:
                        arrived(slot_of(s), c)

    adj = 32 * x
    when(~z_recv, lambda: buf.__setitem__(
        pl.ds(adj // 2, 8), jnp.zeros((8, *buf.shape[1:]), buf.dtype)))
    for offset in (-4, -3, -2, -1, 1, 2, 3, 4):
        when(~exists(me + offset), lambda: lse_far.__setitem__(
            pl.ds(2 * (offset + REACH), 2), jnp.zeros((2, *lse_far.shape[1:]), F32)))

    blocks = cluster_ref.shape[0]
    cluster_copy.wait()
    shift_copy.wait()

    def alive(k, r):
        there = 2 * me + k - 7
        near = jnp.maximum(jnp.minimum(there, blocks - 1), 0)
        same = cluster_ref[near] == cluster_ref[2 * me + r]
        return same & (there == near)

    place = lax.broadcasted_iota(jnp.int32, (1, n), 1)
    within = place % BLOCK
    goal = place - within + (within + shift_ref[...]) % BLOCK
    qrow_ref[...] = goal
    qcol_ref[...] = jnp.broadcast_to(goal.astype(F32), (128, n)).T[:, :1].astype(jnp.int32)

    for own_copy in own_copies:
        own_copy.wait()
    half = lax.broadcasted_iota(jnp.int32, (n, BLOCK), 0)
    lane = lax.broadcasted_iota(jnp.int32, (n, BLOCK), 1)
    q = qcol_ref[...]
    own_scores = []
    for h in range(2):
        s = lax.dot_general(
            buf[pl.ds(first, 2)].reshape(n, -1), buf[first + h], (((1,), (1,)), ((), ())),
            preferred_element_type=F32) * scale
        cell = lane + h * BLOCK
        hit = jnp.sum(jnp.where(q == cell, s, 0.0), axis=1, keepdims=True)
        own_scores.append(hit)
        ok = jnp.concatenate(
            [jnp.full((BLOCK, BLOCK), alive(7 + h, r).astype(jnp.int32), jnp.int32) for r in range(2)], 0) > 0
        scores[7 + h] = jnp.where(ok & (half != cell), s, NEG)
    pos_score[...] = own_scores[0] + own_scores[1]
    m = jnp.maximum(jnp.max(scores[7], axis=1, keepdims=True), jnp.max(scores[8], axis=1, keepdims=True))
    top[...] = m
    total[...] = jnp.sum(jnp.exp(scores[7] - m), axis=1, keepdims=True) + jnp.sum(
        jnp.exp(scores[8] - m), axis=1, keepdims=True)

    def process(block):
        k = block - (2 * g + 1)

        @pl.when((k >= 0) & (k < 16))
        def _():
            far = buf[block]
            for r in range(2):
                part = pl.ds(r * BLOCK, BLOCK)
                s = lax.dot_general(
                    buf[first + r], far,
                    (((1,), (1,)), ((), ())), preferred_element_type=F32) * scale
                s = jnp.where(alive(k, r), s, NEG)
                scores[k, part, :] = s
                old = top[part, :]
                new = jnp.maximum(old, jnp.max(s, axis=1, keepdims=True))
                total[part, :] = total[part, :] * jnp.exp(old - new) + jnp.sum(
                    jnp.exp(s - new), axis=1, keepdims=True)
                top[part, :] = new

    def event(t, kind, i, sends):
        lists = plans[t][0]

        def run():
            if kind == "T":
                when(z_send, lambda: copy(
                    thru.at[pl.ds(i * HALF, HALF), :], thru.at[pl.ds(i * HALF, HALF), :],
                    bs.at[i], trecv.at[i], zto).wait_recv())
            else:
                s = {"X": X_IN, "Y": Y_IN, "Z": Z_IN}[kind][t][i]
                when(z_recv if s < 16 else True, lambda: arrived(slot_of(s), c))
            for link, j in sends:
                when(link_cond(t, link, j), lambda: link_copy(t, lists, link, j, False).start())
            if kind != "T":
                need = c_cond(t, s)
                if need is not False:
                    j = i + {"X": 0, "Y": 12, "Z": 24}[kind]
                    when(need, lambda: c_copy(s, j).start())
        run()

    def step(u, carry):
        spots = [jnp.int32(-1), jnp.int32(-1)]
        for index in range(STEPS):
            for t in range(2):
                for k in range(2):
                    here = (u == index) & (yt == t) & (ct == k)
                    for h, block in enumerate(SCORE[t][k].get(index, ())):
                        spots[h] = jnp.where(here, block + x * (23 - 2 * block), spots[h])
                here = (u == index) & (yt == t)

                @pl.when(here)
                def _():
                    for kind, i, sends in plans[t][2][index]:
                        event(t, kind, i, sends)
                    for k in range(2):
                        blocks_now = SCORE[t][k].get(index, ())
                        if blocks_now:
                            @pl.when(ct == k)
                            def _():
                                for block in blocks_now:
                                    for s in (2 * block, 2 * block + 1):
                                        when(z_recv if s < 16 else True, lambda: arrived(slot_of(s), 1 - c))
        for h in range(2):
            process(spots[h])
        return carry

    lax.fori_loop(0, STEPS, step, 0)

    lse = top[...] + jnp.log(total[...])
    lse_col[...] = lse
    loss = lse - pos_score[...]
    pair = jnp.where(
        lax.broadcasted_iota(jnp.int32, (n, 128), 1) < 8,
        jnp.broadcast_to(lse, (n, 128)), jnp.broadcast_to(loss, (n, 128)))
    turned = pair.T
    for h in range(2):
        row = turned[:1, h * BLOCK:(h + 1) * BLOCK]
        lse_send[h] = row
        lse_far[2 * REACH + h] = row
    loss_ref[...] = turned[8]

    def lse_copy(offset):
        return copy(
            lse_send, lse_far.at[pl.ds(2 * (REACH - offset), 2)], ls.at[REACH + offset], lr.at[REACH - offset],
            me + offset)

    for offset in (-4, 4, -3, 3, -2, 2, -1, 1):
        when(exists(me + offset), lambda: lse_copy(offset).start())

    lows = []
    for r in range(2):
        low = jnp.int32(r)
        for k in range(r, 7 + r):
            low = low + jnp.where(alive(k, r), 0, 1)
        lows.append(low)

    for h in range(2):
        s = scores[7 + h]
        w = jnp.exp(s - lse_col[...]) + jnp.exp(s - lse_far[2 * REACH + h])
        cell = lax.broadcasted_iota(jnp.int32, (n, BLOCK), 1) + h * BLOCK
        line = lax.broadcasted_iota(jnp.int32, (n, BLOCK), 0)
        w = w - (qcol_ref[...] == cell).astype(F32)
        w = w - (qrow_ref[0:1, h * BLOCK:(h + 1) * BLOCK] == line).astype(F32)
        weights[:, h * BLOCK:(h + 1) * BLOCK] = w.astype(jnp.bfloat16)
        scores[7 + h] = jnp.full((n, BLOCK), NEG, F32)

    width = e_hbm.shape[1]

    def own_product(t, carry):
        columns = pl.ds(pl.multiple_of(t * 256, 256), 256)
        grad_ref[:, columns] = jnp.dot(
            weights[:, :2 * BLOCK], buf[pl.ds(first, 2), :, columns].reshape(n, -1), preferred_element_type=F32)
        return carry

    lax.fori_loop(0, width // 256, own_product, 0)

    for r in range(2):
        part = pl.ds(r * BLOCK, BLOCK)
        for j in range(MOST):
            first_exp[part, j * BLOCK:(j + 1) * BLOCK] = jnp.exp(scores[lows[r] + j, part, :] - lse_col[part, :])

    for offset in (-1, 1, -2, 2, -3, 3, -4, 4):
        when(exists(me + offset), lambda: lse_copy(-offset).wait_recv())
    for r in range(2):
        part = pl.ds(r * BLOCK, BLOCK)
        for j in range(MOST):
            k = lows[r] + j
            w = first_exp[part, j * BLOCK:(j + 1) * BLOCK] + jnp.exp(scores[k, part, :] - lse_far[k + 1])
            weights[part, j * BLOCK:(j + 1) * BLOCK] = w.astype(jnp.bfloat16)

    for t in range(width // 256):
        columns = pl.ds(t * 256, 256)
        for r in range(2):
            part = pl.ds(r * BLOCK, BLOCK)
            near = jnp.concatenate([buf[2 * g + 1 + lows[r] + j, :, columns] for j in range(MOST)], 0)
            rest = jnp.dot(weights[part, :], near, preferred_element_type=F32)
            grad_ref[part, columns] = (grad_ref[part, columns] + rest) * scale

    for offset in (-4, 4, -3, 3, -2, 2, -1, 1):
        when(exists(me + offset), lambda: lse_copy(offset).wait_send())
    for t in range(2):
        @pl.when(yt == t)
        def _():
            lists = plans[t][0]
            for link, items in lists.items():
                for i in range(len(items)):
                    when(link_cond(t, link, i), lambda: link_copy(t, lists, link, i, False).wait_send())
            for s, j, need in c_all(t):
                when(need, lambda: c_copy(s, j).wait_send())
            for i in range(2):
                when(z_recv, lambda: back_copy(t, i, False).wait_send())
    for j in range(8):
        copy(rows(16, 0), rows(16, 0), cs.at[32 + j], recv.at[0], cpeer).wait_send()


def solution(mesh):
    row_axis, col_axis = mesh.axis_names
    devices = mesh.shape[row_axis] * mesh.shape[col_axis]
    cols = mesh.shape[col_axis]

    def shards(embeddings, block_cluster, partner_shift):
        rows, width = embeddings.shape
        vmem = pl.BlockSpec(memory_space=pltpu.VMEM)
        hbm = pl.BlockSpec(memory_space=pl.ANY)
        grad, loss = pl.pallas_call(
            functools.partial(kernel, row_axis, col_axis, devices, cols, width ** (-0.5)),
            out_shape=(
                jax.ShapeDtypeStruct((rows, width), F32),
                jax.ShapeDtypeStruct((rows,), F32),
            ),
            in_specs=[hbm, hbm, hbm],
            out_specs=(vmem, vmem),
            scratch_shapes=[
                pltpu.VMEM((24, BLOCK, width), jnp.bfloat16),
                pltpu.VMEM((2 * HALF, width), jnp.bfloat16),
                pltpu.VMEM((16, rows, BLOCK), F32),
                pltpu.VMEM((rows, MOST * BLOCK), F32),
                pltpu.VMEM((rows, MOST * BLOCK), jnp.bfloat16),
                pltpu.VMEM((rows, 1), F32),
                pltpu.VMEM((rows, 1), F32),
                pltpu.VMEM((rows, 1), F32),
                pltpu.VMEM((2, 1, BLOCK), F32),
                pltpu.VMEM((2 * (2 * REACH + 1), 1, BLOCK), F32),
                pltpu.VMEM((rows, 1), F32),
                pltpu.VMEM((rows, 1), jnp.int32),
                pltpu.VMEM((1, rows), jnp.int32),
                pltpu.SMEM(block_cluster.shape, jnp.int32),
                pltpu.VMEM((1, rows), jnp.int32),
                pltpu.SemaphoreType.DMA((96,)),
                pltpu.SemaphoreType.DMA((2,)),
                pltpu.SemaphoreType.DMA((12,)),
                pltpu.SemaphoreType.DMA((12,)),
                pltpu.SemaphoreType.DMA((8,)),
                pltpu.SemaphoreType.DMA((2,)),
                pltpu.SemaphoreType.DMA((40,)),
                pltpu.SemaphoreType.DMA((2 * REACH + 1,)),
                pltpu.SemaphoreType.DMA((2 * REACH + 1,)),
                pltpu.SemaphoreType.DMA((4,)),
            ],
            compiler_params=pltpu.CompilerParams(
                collective_id=0, has_side_effects=True, vmem_limit_bytes=36 * 1024 * 1024
            ),
        )(*[pltpu.with_memory_space_constraint(a, pltpu.HBM) for a in (block_cluster, embeddings, partner_shift.reshape(1, rows))])
        return loss, grad

    in_specs = (P((row_axis, col_axis), None), P(), P((row_axis, col_axis)))
    out_specs = (P((row_axis, col_axis)), P((row_axis, col_axis), None))
    return jax.shard_map(shards, mesh=mesh, in_specs=in_specs, out_specs=out_specs, check_vma=False)
```

```python
import functools

import jax
import jax.numpy as jnp
from jax import lax
from jax.experimental import pallas as pl
from jax.experimental.pallas import tpu as pltpu
from jax.sharding import PartitionSpec as P

BLOCK = 256
MOST = 8
REACH = 4
CHUNK = 128
HALF = 64
NEG = -1e30
F32 = jnp.float32
MESH = pl.DeviceIdType.MESH

X_IN = (
    (40, 34, 41, 35, 36, 37, 38, 39, 32, 33, 10, 11),
    (38, 44, 39, 45, 43, 42, 14, 15, 33, 32, 37, 36),
)
Y_IN = (
    (20, 30, 21, 31, 22, 28, 23, 29, 12, 13, 14, 15),
    (27, 16, 26, 25, 24, 40, 41, 17, 18, 19, 34, 35),
)
Z_IN = (
    (8, 2, 9, 3, 4, 5, 6, 7),
    (6, 12, 7, 13, 11, 8, 10, 9),
)
BACK = ((17, 16), (21, 20))
OWN = (((16, 17, 18, 19), (24, 25, 26, 27)), ((20, 21, 22, 23), (28, 29, 30, 31)))
STEPS = 13


def pairs_of(t, k):
    low = 8 * k + 4 * t + 2
    ready = [[] for _ in range(STEPS)]
    for s in OWN[t][1 - k]:
        ready[0].append(s)
    for i in range(12):
        for s in (X_IN[t][i], Y_IN[t][i]):
            ready[i + 1].append(s)
    for i in range(8):
        ready[i + 3].append(Z_IN[t][i])
    pool, out = [], []
    for u in range(STEPS):
        pool += [s for s in ready[u] if low <= s < low + 32]
        now = []
        while len(pool) >= 2 and len(now) < 2:
            now.append((pool.pop(0), pool.pop(0)))
        out.append(now)
    assert not pool and sum(map(len, out)) == 14
    return out


def events_of(t):
    x_out = [("T", s - (14 if t == 0 else 10)) if s < 16 else ("S", 63 - s) for s in X_IN[1 - t]]
    y_out = [("S", s) for s in Y_IN[1 - t]]
    z_out = [("S", s + 32) for s in Z_IN[t]]
    lists = {"X": x_out, "Y": y_out, "Z": z_out}
    ahead = {"X": 0, "Y": 0, "Z": 0}
    have = {("S", s) for c in range(2) for s in OWN[t][c]}

    def ready():
        out = []
        for link, items in lists.items():
            while ahead[link] < len(items) and items[ahead[link]] in have:
                out.append((link, ahead[link]))
                ahead[link] += 1
        return out

    first = ready()
    steps = []
    for u in range(STEPS):
        now = []
        if u < 12:
            now += [("X", u, ("S", X_IN[t][u])), ("Y", u, ("S", Y_IN[t][u]))]
        if u < 2:
            now.append(("T", u, ("T", u)))
        if 2 <= u < 10:
            now.append(("Z", u - 2, ("S", Z_IN[t][u - 2])))
        done = []
        for kind, i, item in now:
            have.add(item)
            done.append((kind, i, ready()))
        steps.append(done)
    assert all(ahead[link] == len(items) for link, items in lists.items())
    return lists, first, steps


def kernel(
    row_axis, col_axis, devices, cols, scale,
    cluster_hbm, e_hbm, shift_hbm,
    grad_ref, loss_ref,
    buf, thru, scores, first_exp, weights, top, total, lse_col, lse_send, lse_far, pos_score, qcol_ref, qrow_ref,
    cluster_ref, shift_ref,
    recv, trecv, xs, ys, zs, bs, cs, ls, lr, own_sem,
):
    me = lax.axis_index(row_axis) * cols + lax.axis_index(col_axis)
    y = me % 2
    c = me // 2 % 2
    x = me // 4 % 2
    g = 2 * c + y
    yt = (x + y) % 2
    ct = (x + c) % 2
    xpeer = me + 4 - 8 * x
    ypeer = me + 1 - 2 * y
    cpeer = me + 2 - 4 * c
    zto = me + 8 - 16 * x
    zfrom = me - 8 + 16 * x
    z_send = (zto >= 0) & (zto < devices)
    z_recv = (zfrom >= 0) & (zfrom < devices)

    def at(device):
        return (device // cols, device % cols)

    def exists(device):
        return (device >= 0) & (device < devices)

    def when(cond, action):
        if cond is True:
            action()
        else:
            pl.when(cond)(action)

    def both(*conds):
        conds = [cond for cond in conds if cond is not True]
        return functools.reduce(lambda a, b: a & b, conds) if conds else True

    barrier = pltpu.get_barrier_semaphore()
    count = jnp.int32(0)
    for there, device in ((True, xpeer), (True, ypeer), (True, cpeer), (z_send, zto), (z_recv, zfrom)):
        when(there, lambda: pl.semaphore_signal(barrier, inc=1, device_id=at(device), device_id_type=MESH))
        count = count + (1 if there is True else there.astype(jnp.int32))
    pl.semaphore_wait(barrier, count)

    n = e_hbm.shape[0]
    first = 16 + 4 * g

    def slot_of(s):
        return s + x * (47 - 2 * s)

    def rows(slot, half):
        return buf.at[slot, pl.ds(pl.multiple_of(half * HALF, HALF), HALF), :]

    def copy(src, dst, send, receive, device):
        return pltpu.make_async_remote_copy(
            src_ref=src, dst_ref=dst, send_sem=send, recv_sem=receive,
            device_id=at(device), device_id_type=MESH,
        )

    def arrived(slot, half):
        copy(rows(slot, half), rows(slot, half), cs.at[0], recv.at[2 * slot + half], cpeer).wait_recv()

    def mine(s):
        return e_hbm.at[pl.ds(pl.multiple_of((slot_of(s) - 16 - 4 * g) * CHUNK + c * HALF, HALF), HALF), :]

    def source(t, item, own=False):
        kind, s = item
        if kind == "T":
            return thru.at[pl.ds(s * HALF, HALF), :]
        return mine(s) if own else rows(slot_of(s), c)

    def link_copy(t, lists, link, i, own=False):
        item = lists[link][i]
        src = source(t, item, own)
        if link == "X":
            s = X_IN[1 - t][i]
            slot = s + (1 - x) * (47 - 2 * s)
            return copy(src, rows(slot, c), xs.at[i], recv.at[2 * slot + c], xpeer)
        if link == "Y":
            slot = slot_of(Y_IN[1 - t][i])
            return copy(src, rows(slot, c), ys.at[i], recv.at[2 * slot + c], ypeer)
        slot = slot_of(Z_IN[t][i])
        return copy(src, rows(slot, c), zs.at[i], recv.at[2 * slot + c], zto)

    def link_cond(t, link, i):
        if link == "Z":
            return z_send
        if link == "X":
            return z_send if X_IN[1 - t][i] < 16 else True
        return z_recv if Y_IN[1 - t][i] < 16 else True

    def back_copy(t, i, own=False):
        src = source(t, ("S", BACK[t][i]), own)
        return copy(src, thru.at[pl.ds(i * HALF, HALF), :], bs.at[i], trecv.at[i], zfrom)

    def own_half(i, half):
        return e_hbm.at[pl.ds(i * CHUNK + half * HALF, HALF), :]

    def c_own(i, half, j):
        slot = 16 + 4 * g + i
        return copy(own_half(i, half), rows(slot, half), cs.at[32 + j], recv.at[2 * slot + half], cpeer)

    def c_copy(s, j):
        slot = slot_of(s)
        return copy(rows(slot, c), rows(slot, c), cs.at[j], recv.at[2 * slot + c], cpeer)

    def c_cond(t, s):
        low = [8 * k + 4 * t + 2 <= s <= 8 * k + 4 * t + 33 for k in range(2)]
        if low[0] and low[1]:
            need = True
        elif low[0]:
            need = ct == 1
        elif low[1]:
            need = ct == 0
        else:
            return False
        return both(need, z_recv if s < 16 else True)

    plans = [events_of(t) for t in range(2)]

    own_copies = [
        pltpu.make_async_copy(e_hbm.at[pl.ds(h * CHUNK, CHUNK), :], buf.at[first + h], own_sem.at[2 + h]) for h in range(4)]
    cluster_copy = pltpu.make_async_copy(cluster_hbm, cluster_ref, own_sem.at[0])
    shift_copy = pltpu.make_async_copy(shift_hbm, shift_ref, own_sem.at[1])
    for t in range(2):
        for k in range(2):
            @pl.when((yt == t) & (ct == k))
            def _():
                lists, first, _ = plans[t]
                opening = [(link, i) for link, i in first] + [("B", i) for i in range(2)]

                def slot_at(link, i):
                    return BACK[t][i] if link == "B" else lists[link][i][1]

                def send(link, i, own):
                    if link == "B":
                        when(z_recv, lambda: back_copy(t, i, own).start())
                    else:
                        when(link_cond(t, link, i), lambda: link_copy(t, lists, link, i, own).start())

                started = {"X": 0, "Y": 0, "B": 0}
                queue = {link: [i for name, i in opening if name == link] for link in ("X", "Y", "B")}
                plan = {}
                for link, items in queue.items():
                    mine_, other = ([i for i in items if (slot_at(link, i) in OWN[t][k]) == flag] for flag in (True, False))
                    order = []
                    for spot in range(len(items)):
                        take = mine_ if (spot == 0 and mine_) or not other or (mine_ and mine_[0] < other[0]) else other
                        order.append(take.pop(0))
                    plan[link] = order
                leads = []
                for link in ("Y", "X", "B"):
                    while plan[link] and slot_at(link, plan[link][0]) in OWN[t][k]:
                        leads.append((link, plan[link].pop(0)))
                for link, i in leads[:2]:
                    send(link, i, True)
                uses = []
                for link in ("Y", "X", "B", "Y", "X", "B", "Y", "X", "B", "Y", "X", "B", "Y", "Y", "Y", "Y", "X", "X"):
                    if plan[link]:
                        uses.append((link, plan[link].pop(0)))
                assert not any(plan.values())
                order = []
                for s in [s for link, i in [*leads, *uses] for s in [slot_at(link, i)]] + list(OWN[t][k]):
                    if s in OWN[t][k] and s not in order:
                        order.append(s)
                for j, s in enumerate(order):
                    i = slot_of(s) - 16 - 4 * g
                    copy(
                        e_hbm.at[pl.ds(pl.multiple_of(i * CHUNK + (1 - c) * HALF, HALF), HALF), :],
                        rows(slot_of(s), 1 - c), cs.at[32 + j], recv.at[2 * slot_of(s) + 1 - c], cpeer).start()
                for link, i in leads[2:]:
                    send(link, i, True)
                for own_copy in own_copies:
                    own_copy.start()
                cluster_copy.start()
                shift_copy.start()
                for j, s in enumerate(order):
                    copy(mine(s), rows(slot_of(s), c), cs.at[36 + j], recv.at[2 * slot_of(s) + c], cpeer).start()
                waited = set()
                for link, i in uses:
                    s = slot_at(link, i)
                    if s in OWN[t][k]:
                        send(link, i, True)
                        continue
                    if s not in waited:
                        waited.add(s)
                        arrived(slot_of(s), c)
                    send(link, i, False)
                for s in OWN[t][1 - k]:
                    if s not in waited:
                        arrived(slot_of(s), c)

    adj = 32 * x
    when(~z_recv, lambda: buf.__setitem__(
        pl.ds(adj, 16), jnp.zeros((16, *buf.shape[1:]), buf.dtype)))
    for offset in (-4, -3, -2, -1, 1, 2, 3, 4):
        when(~exists(me + offset), lambda: lse_far.__setitem__(
            pl.ds(2 * (offset + REACH), 2), jnp.zeros((2, *lse_far.shape[1:]), F32)))

    blocks = cluster_ref.shape[0]
    cluster_copy.wait()
    shift_copy.wait()

    def alive(k, r):
        there = 2 * me + k - 7
        near = jnp.maximum(jnp.minimum(there, blocks - 1), 0)
        same = cluster_ref[near] == cluster_ref[2 * me + r]
        return same & (there == near)

    place = lax.broadcasted_iota(jnp.int32, (1, n), 1)
    within = place % BLOCK
    goal = place - within + (within + shift_ref[...]) % BLOCK
    qrow_ref[...] = goal
    qcol_ref[...] = jnp.broadcast_to(goal.astype(F32), (128, n)).T[:, :1].astype(jnp.int32)

    for own_copy in own_copies:
        own_copy.wait()
    half = lax.broadcasted_iota(jnp.int32, (n, BLOCK), 0)
    lane = lax.broadcasted_iota(jnp.int32, (n, BLOCK), 1)
    q = qcol_ref[...]
    own_scores = []
    for h in range(2):
        s = lax.dot_general(
            buf[pl.ds(first, 4)].reshape(n, -1), buf[pl.ds(first + 2 * h, 2)].reshape(BLOCK, -1), (((1,), (1,)), ((), ())),
            preferred_element_type=F32) * scale
        cell = lane + h * BLOCK
        hit = jnp.sum(jnp.where(q == cell, s, 0.0), axis=1, keepdims=True)
        own_scores.append(hit)
        ok = jnp.concatenate(
            [jnp.full((BLOCK, BLOCK), alive(7 + h, r).astype(jnp.int32), jnp.int32) for r in range(2)], 0) > 0
        s = jnp.where(ok & (half != cell), s, NEG)
        for i in range(2):
            scores[14 + 2 * h + i] = s[:, i * CHUNK:(i + 1) * CHUNK]
    pos_score[...] = own_scores[0] + own_scores[1]
    near = [scores[14 + i] for i in range(4)]
    m = functools.reduce(jnp.maximum, near)
    top[...] = m
    total[...] = functools.reduce(jnp.add, [jnp.exp(s - m) for s in near])

    def process(slots):
        ks = [slot // 2 - (2 * g + 1) for slot in slots]

        @pl.when(slots[0] >= 0)
        def _():
            far = jnp.concatenate([buf[slot] for slot in slots], 0)
            s = lax.dot_general(
                buf[pl.ds(first, 4)].reshape(n, -1), far,
                (((1,), (1,)), ((), ())), preferred_element_type=F32) * scale
            for r in range(2):
                part = slice(r * BLOCK, (r + 1) * BLOCK)
                halves = [
                    jnp.where(alive(k, r), s[part, i * CHUNK:(i + 1) * CHUNK], NEG) for i, k in enumerate(ks)]
                for slot, value in zip(slots, halves):
                    scores[slot - (4 * g + 2), part, :] = value
                old = top[part, :]
                new = jnp.maximum(old, jnp.maximum(*halves))
                total[part, :] = total[part, :] * jnp.exp(old - new) + (
                    jnp.exp(halves[0] - new) + jnp.exp(halves[1] - new))
                top[part, :] = new

    def event(t, kind, i, sends):
        lists = plans[t][0]

        def run():
            if kind == "T":
                when(z_send, lambda: copy(
                    thru.at[pl.ds(i * HALF, HALF), :], thru.at[pl.ds(i * HALF, HALF), :],
                    bs.at[i], trecv.at[i], zto).wait_recv())
            else:
                s = {"X": X_IN, "Y": Y_IN, "Z": Z_IN}[kind][t][i]
                when(z_recv if s < 16 else True, lambda: arrived(slot_of(s), c))
            for link, j in sends:
                when(link_cond(t, link, j), lambda: link_copy(t, lists, link, j, False).start())
            if kind != "T":
                need = c_cond(t, s)
                if need is not False:
                    j = i + {"X": 0, "Y": 12, "Z": 24}[kind]
                    when(need, lambda: c_copy(s, j).start())
        run()

    pairs = [[pairs_of(t, k) for k in range(2)] for t in range(2)]

    def spent(t, u):
        lists, first_sends, steps = plans[t]
        started = {item: -1 for item in first_sends}
        started.update({item: v for v, events in enumerate(steps) for _, _, sends in events for item in sends})
        for (link, i), v in started.items():
            due = min(max(i, v) + 3 if link != "Z" else v + 4, STEPS)
            if due == u:
                when(link_cond(t, link, i), lambda: link_copy(t, lists, link, i, False).wait_send())
        for v, events in enumerate(steps):
            if min(v + 2, STEPS) == u:
                for kind, i, _ in events:
                    if kind != "T":
                        s = {"X": X_IN, "Y": Y_IN, "Z": Z_IN}[kind][t][i]
                        need = c_cond(t, s)
                        if need is not False:
                            when(need, lambda: c_copy(s, i + {"X": 0, "Y": 12, "Z": 24}[kind]).wait_send())
        if u == 3:
            for i in range(2):
                when(z_recv, lambda: back_copy(t, i, False).wait_send())
            for j in range(8):
                copy(rows(16, 0), rows(16, 0), cs.at[32 + j], recv.at[0], cpeer).wait_send()

    for u in range(STEPS):
        for t in range(2):
            @pl.when(yt == t)
            def _():
                for kind, i, sends in plans[t][2][u]:
                    event(t, kind, i, sends)
                spent(t, u)
                for k in range(2):
                    now = pairs[t][k][u]
                    if now:
                        @pl.when(ct == k)
                        def _():
                            for s in [s for pair in now for s in pair]:
                                when(z_recv if s < 16 else True, lambda: arrived(slot_of(s), 1 - c))
        for h in range(max(len(pairs[t][k][u]) for t in range(2) for k in range(2))):
            spots = [jnp.int32(-1), jnp.int32(-1)]
            for t in range(2):
                for k in range(2):
                    if h < len(pairs[t][k][u]):
                        here = (yt == t) & (ct == k)
                        spots = [jnp.where(here, slot_of(s), spot) for s, spot in zip(pairs[t][k][u][h], spots)]
            process(spots)

    eye = lax.broadcasted_iota(jnp.int32, (CHUNK, CHUNK), 0) == lax.broadcasted_iota(jnp.int32, (CHUNK, CHUNK), 1)

    def as_row(column):
        return jnp.sum(jnp.where(eye, jnp.broadcast_to(column, (CHUNK, CHUNK)), 0.0), axis=0, keepdims=True)

    lse_rows = []
    for i in range(n // CHUNK):
        part = slice(i * CHUNK, (i + 1) * CHUNK)
        m = jnp.max(top[part, :], axis=1, keepdims=True)
        t = jnp.sum(total[part, :] * jnp.exp(top[part, :] - m), axis=1, keepdims=True)
        lse_rows.append(as_row(m) + jnp.log(as_row(t)))
        lse_col[part, :] = m + jnp.log(t)
    for h in range(2):
        row = jnp.concatenate(lse_rows[2 * h:2 * h + 2], 1)
        lse_send[h] = row
        lse_far[2 * REACH + h] = row

    def lse_copy(offset):
        return copy(
            lse_send, lse_far.at[pl.ds(2 * (REACH - offset), 2)], ls.at[REACH + offset], lr.at[REACH - offset],
            me + offset)

    for offset in (-4, 4, -3, 3, -2, 2, -1, 1):
        when(exists(me + offset), lambda: lse_copy(offset).start())

    loss_ref[...] = jnp.concatenate([row - as_row(pos_score[i * CHUNK:(i + 1) * CHUNK, :]) for i, row in enumerate(lse_rows)], 1)[0]

    lows = []
    for r in range(2):
        low = jnp.int32(r)
        for k in range(r, 7 + r):
            low = low + jnp.where(alive(k, r), 0, 1)
        lows.append(low)

    for h in range(2):
        s = jnp.concatenate([scores[14 + 2 * h + i] for i in range(2)], 1)
        w = jnp.exp(s - lse_col[...]) + jnp.exp(s - lse_far[2 * REACH + h])
        cell = lax.broadcasted_iota(jnp.int32, (n, BLOCK), 1) + h * BLOCK
        line = lax.broadcasted_iota(jnp.int32, (n, BLOCK), 0)
        w = w - (qcol_ref[...] == cell).astype(F32)
        w = w - (qrow_ref[0:1, h * BLOCK:(h + 1) * BLOCK] == line).astype(F32)
        weights[:, h * BLOCK:(h + 1) * BLOCK] = w.astype(jnp.bfloat16)
        for i in range(2):
            scores[14 + 2 * h + i] = jnp.full((n, CHUNK), NEG, F32)

    width = e_hbm.shape[1]

    def own_product(t, carry):
        columns = pl.ds(pl.multiple_of(t * 256, 256), 256)
        grad_ref[:, columns] = jnp.dot(
            weights[:, :2 * BLOCK], buf[pl.ds(first, 4), :, columns].reshape(n, -1), preferred_element_type=F32)
        return carry

    lax.fori_loop(0, width // 256, own_product, 0)

    for r in range(2):
        part = pl.ds(r * BLOCK, BLOCK)
        for j in range(2 * MOST):
            first_exp[part, j * CHUNK:(j + 1) * CHUNK] = jnp.exp(scores[2 * lows[r] + j, part, :] - lse_col[part, :])

    for offset in (-1, 1, -2, 2, -3, 3, -4, 4):
        when(exists(me + offset), lambda: lse_copy(-offset).wait_recv())
    for r in range(2):
        part = pl.ds(r * BLOCK, BLOCK)
        for j in range(MOST):
            far = lse_far[lows[r] + j + 1]
            for i in range(2):
                spot = slice((2 * j + i) * CHUNK, (2 * j + i + 1) * CHUNK)
                w = first_exp[part, spot] + jnp.exp(
                    scores[2 * lows[r] + 2 * j + i, part, :] - far[:, i * CHUNK:(i + 1) * CHUNK])
                weights[part, spot] = w.astype(jnp.bfloat16)

    for t in range(width // 256):
        columns = pl.ds(t * 256, 256)
        for r in range(2):
            part = pl.ds(r * BLOCK, BLOCK)
            near = jnp.concatenate([buf[4 * g + 2 + 2 * lows[r] + j, :, columns] for j in range(2 * MOST)], 0)
            rest = jnp.dot(weights[part, :], near, preferred_element_type=F32)
            grad_ref[part, columns] = (grad_ref[part, columns] + rest) * scale

    for offset in (-4, 4, -3, 3, -2, 2, -1, 1):
        when(exists(me + offset), lambda: lse_copy(offset).wait_send())
    for t in range(2):
        @pl.when(yt == t)
        def _():
            spent(t, STEPS)


def solution(mesh):
    row_axis, col_axis = mesh.axis_names
    devices = mesh.shape[row_axis] * mesh.shape[col_axis]
    cols = mesh.shape[col_axis]

    def shards(embeddings, block_cluster, partner_shift):
        rows, width = embeddings.shape
        vmem = pl.BlockSpec(memory_space=pltpu.VMEM)
        hbm = pl.BlockSpec(memory_space=pl.ANY)
        grad, loss = pl.pallas_call(
            functools.partial(kernel, row_axis, col_axis, devices, cols, width ** (-0.5)),
            out_shape=(
                jax.ShapeDtypeStruct((rows, width), F32),
                jax.ShapeDtypeStruct((rows,), F32),
            ),
            in_specs=[hbm, hbm, hbm],
            out_specs=(vmem, vmem),
            scratch_shapes=[
                pltpu.VMEM((48, CHUNK, width), jnp.bfloat16),
                pltpu.VMEM((2 * HALF, width), jnp.bfloat16),
                pltpu.VMEM((32, rows, CHUNK), F32),
                pltpu.VMEM((rows, MOST * BLOCK), F32),
                pltpu.VMEM((rows, MOST * BLOCK), jnp.bfloat16),
                pltpu.VMEM((rows, CHUNK), F32),
                pltpu.VMEM((rows, CHUNK), F32),
                pltpu.VMEM((rows, 1), F32),
                pltpu.VMEM((2, 1, BLOCK), F32),
                pltpu.VMEM((2 * (2 * REACH + 1), 1, BLOCK), F32),
                pltpu.VMEM((rows, 1), F32),
                pltpu.VMEM((rows, 1), jnp.int32),
                pltpu.VMEM((1, rows), jnp.int32),
                pltpu.SMEM(block_cluster.shape, jnp.int32),
                pltpu.VMEM((1, rows), jnp.int32),
                pltpu.SemaphoreType.DMA((96,)),
                pltpu.SemaphoreType.DMA((2,)),
                pltpu.SemaphoreType.DMA((12,)),
                pltpu.SemaphoreType.DMA((12,)),
                pltpu.SemaphoreType.DMA((8,)),
                pltpu.SemaphoreType.DMA((2,)),
                pltpu.SemaphoreType.DMA((40,)),
                pltpu.SemaphoreType.DMA((2 * REACH + 1,)),
                pltpu.SemaphoreType.DMA((2 * REACH + 1,)),
                pltpu.SemaphoreType.DMA((6,)),
            ],
            compiler_params=pltpu.CompilerParams(
                collective_id=0, has_side_effects=True, vmem_limit_bytes=36 * 1024 * 1024
            ),
        )(*[pltpu.with_memory_space_constraint(a, pltpu.HBM) for a in (block_cluster, embeddings, partner_shift.reshape(1, rows))])
        return loss, grad

    in_specs = (P((row_axis, col_axis), None), P(), P((row_axis, col_axis)))
    out_specs = (P((row_axis, col_axis)), P((row_axis, col_axis), None))
    return jax.shard_map(shards, mesh=mesh, in_specs=in_specs, out_specs=out_specs, check_vma=False)
```

```python
import functools

import jax
import jax.numpy as jnp
from jax import lax
from jax.experimental import pallas as pl
from jax.experimental.pallas import tpu as pltpu
from jax.sharding import PartitionSpec as P

BLOCK = 256
MOST = 8
REACH = 4
CHUNK = 128
HALF = 64
NEG = -1e30
F32 = jnp.float32
MESH = pl.DeviceIdType.MESH

X_IN = (
    (40, 34, 41, 35, 36, 37, 38, 39, 32, 33, 10, 11),
    (38, 44, 39, 45, 43, 42, 14, 15, 33, 32, 37, 36),
)
Y_IN = (
    (20, 30, 21, 31, 22, 28, 23, 29, 12, 13, 14, 15),
    (27, 16, 26, 25, 24, 40, 41, 17, 18, 19, 34, 35),
)
Z_IN = (
    (8, 2, 9, 3, 4, 5, 6, 7),
    (6, 12, 7, 13, 11, 8, 10, 9),
)
BACK = ((17, 16), (21, 20))
OWN = (((16, 17, 18, 19), (24, 25, 26, 27)), ((20, 21, 22, 23), (28, 29, 30, 31)))
STEPS = 13


def pairs_of(t, k):
    low = 8 * k + 4 * t + 2
    ready = [[] for _ in range(STEPS)]
    for s in OWN[t][1 - k]:
        ready[0].append(s)
    for i in range(12):
        for s in (X_IN[t][i], Y_IN[t][i]):
            ready[i + 1].append(s)
    for i in range(8):
        ready[i // 2 * 2 + 4].append(Z_IN[t][i])
    pool, out = [], []
    for u in range(STEPS):
        pool += [s for s in ready[u] if low <= s < low + 32]
        now = []
        while len(pool) >= 2 and len(now) < 2:
            now.append((pool.pop(0), pool.pop(0)))
        out.append(now)
    assert not pool and sum(map(len, out)) == 14
    return out


def events_of(t):
    x_out = [("T", s - (14 if t == 0 else 10)) if s < 16 else ("S", 63 - s) for s in X_IN[1 - t]]
    y_out = [("S", s) for s in Y_IN[1 - t]]
    z_out = [("S", s + 32) for s in Z_IN[t]]
    lists = {"X": x_out, "Y": y_out, "Z": z_out}
    ahead = {"X": 0, "Y": 0, "Z": 0}
    have = {("S", s) for c in range(2) for s in OWN[t][c]}

    def ready():
        out = []
        for link, items in lists.items():
            while ahead[link] < len(items) and items[ahead[link]] in have:
                out.append((link, ahead[link]))
                ahead[link] += 1
        return out

    first = ready()
    steps = []
    for u in range(STEPS):
        now = []
        if u < 12:
            now += [("X", u, ("S", X_IN[t][u])), ("Y", u, ("S", Y_IN[t][u]))]
        if u == 1:
            now.append(("T", 0, ("T", 0), ("T", 1)))
        if u in (3, 5, 7, 9):
            now.append(("Z", (u - 3) // 2, *[("S", s) for s in Z_IN[t][u - 3:u - 1]]))
        done = []
        for kind, i, *items in now:
            have.update(items)
            done.append((kind, i, ready()))
        steps.append(done)
    assert all(ahead[link] == len(items) for link, items in lists.items())
    return lists, first, steps


def kernel(
    row_axis, col_axis, devices, cols, scale,
    cluster_hbm, e_hbm, shift_hbm,
    grad_ref, loss_ref,
    buf, thru, scores, first_exp, weights, top, total, lse_col, lse_send, lse_far, pos_score, qcol_ref, qrow_ref,
    cluster_ref, shift_ref,
    rx, ry, rz, rt, rc, ro, sent, ls, lr, own_sem,
):
    me = lax.axis_index(row_axis) * cols + lax.axis_index(col_axis)
    y = me % 2
    c = me // 2 % 2
    x = me // 4 % 2
    g = 2 * c + y
    yt = (x + y) % 2
    ct = (x + c) % 2
    xpeer = me + 4 - 8 * x
    ypeer = me + 1 - 2 * y
    cpeer = me + 2 - 4 * c
    zto = me + 8 - 16 * x
    zfrom = me - 8 + 16 * x
    z_send = (zto >= 0) & (zto < devices)
    z_recv = (zfrom >= 0) & (zfrom < devices)

    def at(device):
        return (device // cols, device % cols)

    def exists(device):
        return (device >= 0) & (device < devices)

    def when(cond, action):
        if cond is True:
            action()
        else:
            pl.when(cond)(action)

    def both(*conds):
        conds = [cond for cond in conds if cond is not True]
        return functools.reduce(lambda a, b: a & b, conds) if conds else True

    barrier = pltpu.get_barrier_semaphore()
    count = jnp.int32(0)
    for there, device in ((True, xpeer), (True, ypeer), (True, cpeer), (z_send, zto), (z_recv, zfrom)):
        when(there, lambda: pl.semaphore_signal(barrier, inc=1, device_id=at(device), device_id_type=MESH))
        count = count + (1 if there is True else there.astype(jnp.int32))
    pl.semaphore_wait(barrier, count)

    n = e_hbm.shape[0] * CHUNK
    first = 16 + 4 * g

    def slot_of(s):
        return s + x * (47 - 2 * s)

    def rows(slot, half):
        return buf.at[slot, pl.ds(pl.multiple_of(half * HALF, HALF), HALF), :]

    def copy(src, dst, send, receive, device):
        return pltpu.make_async_remote_copy(
            src_ref=src, dst_ref=dst, send_sem=send, recv_sem=receive,
            device_id=at(device), device_id_type=MESH,
        )

    def some(count):
        return buf.at[pl.ds(0, count), pl.ds(0, HALF), :]

    def got(sem, count):
        copy(some(count), some(count), sent.at[0], sem, cpeer).wait_recv()

    def gone(sem, count):
        if count:
            copy(some(count), some(count), sem, rt.at[0], cpeer).wait_send()

    def mine(s, half):
        return e_hbm.at[slot_of(s) - first, pl.ds(pl.multiple_of(half * HALF, HALF), HALF), :]

    def source(item, own):
        kind, s = item
        if kind == "T":
            return thru.at[pl.ds(s * HALF, HALF), :]
        return mine(s, c) if own else rows(slot_of(s), c)

    def link_cond(t, link, i):
        if link in "BZ":
            return "R" if link == "B" else "S"
        if link == "X":
            return "S" if X_IN[1 - t][i] < 16 else True
        return "R" if Y_IN[1 - t][i] < 16 else True

    def holds(cond):
        return {"S": z_send, "R": z_recv, True: True}[cond]

    def link_send(t, lists, link, i, own=False):
        cond = link_cond(t, link, i)
        sem = sent.at[{True: 0, "S": 1, "R": 2}[cond]]
        if link == "B":
            todo = copy(source(("S", BACK[t][i]), own), thru.at[pl.ds(i * HALF, HALF), :], sem, rt.at[0], zfrom)
        elif link == "X":
            s = X_IN[1 - t][i]
            todo = copy(source(lists[link][i], own), rows(s + (1 - x) * (47 - 2 * s), c), sem, rx.at[i], xpeer)
        elif link == "Y":
            todo = copy(source(lists[link][i], own), rows(slot_of(Y_IN[1 - t][i]), c), sem, ry.at[i], ypeer)
        else:
            todo = copy(source(lists[link][i], own), rows(slot_of(Z_IN[t][i]), c), sem, rz.at[i // 2], zto)
        when(holds(cond), lambda: todo.start())

    pairs = [[pairs_of(t, k) for k in range(2)] for t in range(2)]

    def pair_of(t, k, s):
        return [s in pair for now in pairs[t][k] for pair in now].index(True)

    def c_need(t, s):
        return [k for k in range(2) if 8 * (1 - k) + 4 * t + 2 <= s <= 8 * (1 - k) + 4 * t + 33]

    def c_send(t, s):
        for k in c_need(t, s):
            sem = sent.at[2 if s < 16 else 3]
            spot = rows(slot_of(s), c)
            when(both(ct == k, z_recv if s < 16 else True), lambda: copy(
                spot, spot, sem, rc.at[pair_of(t, 1 - k, s)], cpeer).start())

    plans = [events_of(t) for t in range(2)]

    own_copy = pltpu.make_async_copy(e_hbm, buf.at[pl.ds(first, 4)], own_sem.at[2])
    cluster_copy = pltpu.make_async_copy(cluster_hbm, cluster_ref, own_sem.at[0])
    shift_copy = pltpu.make_async_copy(shift_hbm, shift_ref, own_sem.at[1])
    for t in range(2):
        for k in range(2):
            @pl.when((yt == t) & (ct == k))
            def _():
                lists, first, _ = plans[t]
                opening = [(link, i) for link, i in first] + [("B", i) for i in range(2)]

                def slot_at(link, i):
                    return BACK[t][i] if link == "B" else lists[link][i][1]

                def send(link, i, own):
                    link_send(t, lists, link, i, own)

                queue = {link: [i for name, i in opening if name == link] for link in ("X", "Y", "B")}
                plan = {}
                for link, items in queue.items():
                    mine_, other = ([i for i in items if (slot_at(link, i) in OWN[t][k]) == flag] for flag in (True, False))
                    order = []
                    for spot in range(len(items)):
                        take = mine_ if (spot == 0 and mine_) or not other or (mine_ and mine_[0] < other[0]) else other
                        order.append(take.pop(0))
                    plan[link] = order
                leads = []
                for link in ("Y", "X", "B"):
                    while plan[link] and slot_at(link, plan[link][0]) in OWN[t][k]:
                        leads.append((link, plan[link].pop(0)))
                for link, i in leads[:2]:
                    send(link, i, True)
                uses = []
                for link in ("Y", "X", "B", "Y", "X", "B", "Y", "X", "B", "Y", "X", "B", "Y", "Y", "Y", "Y", "X", "X"):
                    if plan[link]:
                        uses.append((link, plan[link].pop(0)))
                assert not any(plan.values())
                order = []
                for s in [s for link, i in [*leads, *uses] for s in [slot_at(link, i)]] + list(OWN[t][k]):
                    if s in OWN[t][k] and s not in order:
                        order.append(s)
                for s in order:
                    copy(
                        mine(s, 1 - c), rows(slot_of(s), 1 - c), sent.at[3], ro.at[OWN[t][k].index(s)],
                        cpeer).start()
                for link, i in leads[2:]:
                    send(link, i, True)
                own_copy.start()
                cluster_copy.start()
                shift_copy.start()
                for s in order:
                    copy(
                        mine(s, c), rows(slot_of(s), c), sent.at[3], rc.at[pair_of(t, 1 - k, s)], cpeer).start()
                waited = set()
                for link, i in uses:
                    s = slot_at(link, i)
                    if s in OWN[t][k]:
                        send(link, i, True)
                        continue
                    if s not in waited:
                        waited.add(s)
                        got(ro.at[OWN[t][1 - k].index(s)], 1)
                    send(link, i, False)
                for s in OWN[t][1 - k]:
                    if s not in waited:
                        got(ro.at[OWN[t][1 - k].index(s)], 1)

    adj = 32 * x
    when(~z_recv, lambda: buf.__setitem__(
        pl.ds(adj, 16), jnp.zeros((16, *buf.shape[1:]), buf.dtype)))
    for offset in (-4, -3, -2, -1, 1, 2, 3, 4):
        when(~exists(me + offset), lambda: lse_far.__setitem__(
            pl.ds(2 * (offset + REACH), 2), jnp.zeros((2, *lse_far.shape[1:]), F32)))

    blocks = cluster_ref.shape[0]
    cluster_copy.wait()
    shift_copy.wait()

    def alive(k, r):
        there = 2 * me + k - 7
        near = jnp.maximum(jnp.minimum(there, blocks - 1), 0)
        same = cluster_ref[near] == cluster_ref[2 * me + r]
        return same & (there == near)

    place = lax.broadcasted_iota(jnp.int32, (1, n), 1)
    within = place % BLOCK
    goal = place - within + (within + shift_ref[...]) % BLOCK
    qrow_ref[...] = goal
    qcol_ref[...] = jnp.broadcast_to(goal.astype(F32), (128, n)).T[:, :1].astype(jnp.int32)

    own_copy.wait()
    half = lax.broadcasted_iota(jnp.int32, (n, BLOCK), 0)
    lane = lax.broadcasted_iota(jnp.int32, (n, BLOCK), 1)
    q = qcol_ref[...]
    own_scores = []
    for h in range(2):
        s = lax.dot_general(
            buf[pl.ds(first, 4)].reshape(n, -1), buf[pl.ds(first + 2 * h, 2)].reshape(BLOCK, -1), (((1,), (1,)), ((), ())),
            preferred_element_type=F32) * scale
        cell = lane + h * BLOCK
        hit = jnp.sum(jnp.where(q == cell, s, 0.0), axis=1, keepdims=True)
        own_scores.append(hit)
        ok = jnp.concatenate(
            [jnp.full((BLOCK, BLOCK), alive(7 + h, r).astype(jnp.int32), jnp.int32) for r in range(2)], 0) > 0
        s = jnp.where(ok & (half != cell), s, NEG)
        for i in range(2):
            scores[14 + 2 * h + i] = s[:, i * CHUNK:(i + 1) * CHUNK]
    pos_score[...] = own_scores[0] + own_scores[1]
    near = [scores[14 + i] for i in range(4)]
    m = functools.reduce(jnp.maximum, near)
    top[...] = m
    total[...] = functools.reduce(jnp.add, [jnp.exp(s - m) for s in near])

    def process(slots):
        ks = [slot // 2 - (2 * g + 1) for slot in slots]

        @pl.when(slots[0] >= 0)
        def _():
            far = jnp.concatenate([buf[slot] for slot in slots], 0)
            s = lax.dot_general(
                buf[pl.ds(first, 4)].reshape(n, -1), far,
                (((1,), (1,)), ((), ())), preferred_element_type=F32) * scale
            for r in range(2):
                part = slice(r * BLOCK, (r + 1) * BLOCK)
                halves = [
                    jnp.where(alive(k, r), s[part, i * CHUNK:(i + 1) * CHUNK], NEG) for i, k in enumerate(ks)]
                for slot, value in zip(slots, halves):
                    scores[slot - (4 * g + 2), part, :] = value
                old = top[part, :]
                new = jnp.maximum(old, jnp.maximum(*halves))
                total[part, :] = total[part, :] * jnp.exp(old - new) + (
                    jnp.exp(halves[0] - new) + jnp.exp(halves[1] - new))
                top[part, :] = new

    def event(t, kind, i, sends):
        lists = plans[t][0]
        if kind == "T":
            when(z_send, lambda: got(rt.at[0], 2))
            slots = []
        elif kind == "Z":
            when(z_recv, lambda: got(rz.at[i], 2))
            slots = Z_IN[t][2 * i:2 * i + 2]
        else:
            slots = [{"X": X_IN, "Y": Y_IN}[kind][t][i]]
            sem = {"X": rx, "Y": ry}[kind].at[i]
            when(z_recv if slots[0] < 16 else True, lambda: got(sem, 1))
        for link, j in sends:
            link_send(t, lists, link, j)
        for s in slots:
            c_send(t, s)

    def c_wait(t, k, pair):
        sem = rc.at[pair_of(t, k, pair[0])]
        count = sum(s >= 16 for s in pair)
        if count == 2:
            got(sem, 2)
            return
        when(z_recv, lambda: got(sem, 2))
        if count:
            when(~z_recv, lambda: got(sem, 1))

    for u in range(STEPS):
        for t in range(2):
            @pl.when(yt == t)
            def _():
                for kind, i, sends in plans[t][2][u]:
                    event(t, kind, i, sends)
                for k in range(2):
                    now = pairs[t][k][u]
                    if now:
                        @pl.when(ct == k)
                        def _():
                            for pair in now:
                                c_wait(t, k, pair)
        for h in range(max(len(pairs[t][k][u]) for t in range(2) for k in range(2))):
            spots = [jnp.int32(-1), jnp.int32(-1)]
            for t in range(2):
                for k in range(2):
                    if h < len(pairs[t][k][u]):
                        here = (yt == t) & (ct == k)
                        spots = [jnp.where(here, slot_of(s), spot) for s, spot in zip(pairs[t][k][u][h], spots)]
            process(spots)

    eye = lax.broadcasted_iota(jnp.int32, (CHUNK, CHUNK), 0) == lax.broadcasted_iota(jnp.int32, (CHUNK, CHUNK), 1)

    def as_row(column):
        return jnp.sum(jnp.where(eye, jnp.broadcast_to(column, (CHUNK, CHUNK)), 0.0), axis=0, keepdims=True)

    lse_rows = []
    for i in range(n // CHUNK):
        part = slice(i * CHUNK, (i + 1) * CHUNK)
        m = jnp.max(top[part, :], axis=1, keepdims=True)
        t = jnp.sum(total[part, :] * jnp.exp(top[part, :] - m), axis=1, keepdims=True)
        lse_rows.append(as_row(m) + jnp.log(as_row(t)))
        lse_col[part, :] = m + jnp.log(t)
    for h in range(2):
        row = jnp.concatenate(lse_rows[2 * h:2 * h + 2], 1)
        lse_send[h] = row
        lse_far[2 * REACH + h] = row

    def lse_copy(offset):
        return copy(
            lse_send, lse_far.at[pl.ds(2 * (REACH - offset), 2)], ls.at[0], lr.at[0], me + offset)

    for offset in (-4, 4, -3, 3, -2, 2, -1, 1):
        when(exists(me + offset), lambda: lse_copy(offset).start())

    loss_ref[...] = jnp.concatenate([row - as_row(pos_score[i * CHUNK:(i + 1) * CHUNK, :]) for i, row in enumerate(lse_rows)], 1)[0]

    lows = []
    for r in range(2):
        low = jnp.int32(r)
        for k in range(r, 7 + r):
            low = low + jnp.where(alive(k, r), 0, 1)
        lows.append(low)

    for h in range(2):
        s = jnp.concatenate([scores[14 + 2 * h + i] for i in range(2)], 1)
        w = jnp.exp(s - lse_col[...]) + jnp.exp(s - lse_far[2 * REACH + h])
        cell = lax.broadcasted_iota(jnp.int32, (n, BLOCK), 1) + h * BLOCK
        line = lax.broadcasted_iota(jnp.int32, (n, BLOCK), 0)
        w = w - (qcol_ref[...] == cell).astype(F32)
        w = w - (qrow_ref[0:1, h * BLOCK:(h + 1) * BLOCK] == line).astype(F32)
        weights[:, h * BLOCK:(h + 1) * BLOCK] = w.astype(jnp.bfloat16)
        for i in range(2):
            scores[14 + 2 * h + i] = jnp.full((n, CHUNK), NEG, F32)

    width = e_hbm.shape[2]

    def own_product(t, carry):
        columns = pl.ds(pl.multiple_of(t * 256, 256), 256)
        grad_ref[:, columns] = jnp.dot(
            weights[:, :2 * BLOCK], buf[pl.ds(first, 4), :, columns].reshape(n, -1), preferred_element_type=F32)
        return carry

    lax.fori_loop(0, width // 256, own_product, 0)

    for r in range(2):
        part = pl.ds(r * BLOCK, BLOCK)
        for j in range(2 * MOST):
            first_exp[part, j * CHUNK:(j + 1) * CHUNK] = jnp.exp(scores[2 * lows[r] + j, part, :] - lse_col[part, :])

    partners = jnp.minimum(me, REACH) + jnp.minimum(devices - 1 - me, REACH)

    def lse_all(count):
        spot = lse_far.at[pl.ds(0, 2 * count)]
        return copy(spot, spot, ls.at[0], lr.at[0], cpeer)

    for count in range(REACH, 2 * REACH + 1):
        when(partners == count, lambda: lse_all(count).wait_recv())
    for r in range(2):
        part = pl.ds(r * BLOCK, BLOCK)
        for j in range(MOST):
            far = lse_far[lows[r] + j + 1]
            for i in range(2):
                spot = slice((2 * j + i) * CHUNK, (2 * j + i + 1) * CHUNK)
                w = first_exp[part, spot] + jnp.exp(
                    scores[2 * lows[r] + 2 * j + i, part, :] - far[:, i * CHUNK:(i + 1) * CHUNK])
                weights[part, spot] = w.astype(jnp.bfloat16)

    for t in range(width // 256):
        columns = pl.ds(t * 256, 256)
        for r in range(2):
            part = pl.ds(r * BLOCK, BLOCK)
            near = jnp.concatenate([buf[4 * g + 2 + 2 * lows[r] + j, :, columns] for j in range(2 * MOST)], 0)
            rest = jnp.dot(weights[part, :], near, preferred_element_type=F32)
            grad_ref[part, columns] = (grad_ref[part, columns] + rest) * scale

    for count in range(REACH, 2 * REACH + 1):
        when(partners == count, lambda: lse_all(count).wait_send())
    for t in range(2):
        conds = [link_cond(t, link, i) for link, items in plans[t][0].items() for i in range(len(items))] + ["R", "R"]
        arrivals = [s for steps in (X_IN[t], Y_IN[t], Z_IN[t]) for s in steps]
        for k in range(2):
            @pl.when((yt == t) & (ct == k))
            def _():
                relayed = [s for s in arrivals if k in c_need(t, s)]
                gone(sent.at[0], conds.count(True))
                when(z_send, lambda: gone(sent.at[1], conds.count("S")))
                when(z_recv, lambda: gone(sent.at[2], conds.count("R") + sum(s < 16 for s in relayed)))
                gone(sent.at[3], 8 + sum(s >= 16 for s in relayed))


def solution(mesh):
    row_axis, col_axis = mesh.axis_names
    devices = mesh.shape[row_axis] * mesh.shape[col_axis]
    cols = mesh.shape[col_axis]

    def shards(embeddings, block_cluster, partner_shift):
        rows, width = embeddings.shape
        vmem = pl.BlockSpec(memory_space=pltpu.VMEM)
        hbm = pl.BlockSpec(memory_space=pl.ANY)
        grad, loss = pl.pallas_call(
            functools.partial(kernel, row_axis, col_axis, devices, cols, width ** (-0.5)),
            out_shape=(
                jax.ShapeDtypeStruct((rows, width), F32),
                jax.ShapeDtypeStruct((rows,), F32),
            ),
            in_specs=[hbm, hbm, hbm],
            out_specs=(vmem, vmem),
            scratch_shapes=[
                pltpu.VMEM((48, CHUNK, width), jnp.bfloat16),
                pltpu.VMEM((2 * HALF, width), jnp.bfloat16),
                pltpu.VMEM((32, rows, CHUNK), F32),
                pltpu.VMEM((rows, MOST * BLOCK), F32),
                pltpu.VMEM((rows, MOST * BLOCK), jnp.bfloat16),
                pltpu.VMEM((rows, CHUNK), F32),
                pltpu.VMEM((rows, CHUNK), F32),
                pltpu.VMEM((rows, 1), F32),
                pltpu.VMEM((2, 1, BLOCK), F32),
                pltpu.VMEM((2 * (2 * REACH + 1), 1, BLOCK), F32),
                pltpu.VMEM((rows, 1), F32),
                pltpu.VMEM((rows, 1), jnp.int32),
                pltpu.VMEM((1, rows), jnp.int32),
                pltpu.SMEM(block_cluster.shape, jnp.int32),
                pltpu.VMEM((1, rows), jnp.int32),
                pltpu.SemaphoreType.DMA((12,)),
                pltpu.SemaphoreType.DMA((12,)),
                pltpu.SemaphoreType.DMA((4,)),
                pltpu.SemaphoreType.DMA((1,)),
                pltpu.SemaphoreType.DMA((14,)),
                pltpu.SemaphoreType.DMA((4,)),
                pltpu.SemaphoreType.DMA((4,)),
                pltpu.SemaphoreType.DMA((1,)),
                pltpu.SemaphoreType.DMA((1,)),
                pltpu.SemaphoreType.DMA((3,)),
            ],
            compiler_params=pltpu.CompilerParams(
                collective_id=0, has_side_effects=True, vmem_limit_bytes=36 * 1024 * 1024
            ),
        )(*[pltpu.with_memory_space_constraint(a, pltpu.HBM) for a in (
            block_cluster, embeddings.reshape(rows // CHUNK, CHUNK, width), partner_shift.reshape(1, rows))])
        return loss, grad

    in_specs = (P((row_axis, col_axis), None), P(), P((row_axis, col_axis)))
    out_specs = (P((row_axis, col_axis)), P((row_axis, col_axis), None))
    return jax.shard_map(shards, mesh=mesh, in_specs=in_specs, out_specs=out_specs, check_vma=False)
```

```python
import functools

import jax
import jax.numpy as jnp
from jax import lax
from jax.experimental import pallas as pl
from jax.experimental.pallas import tpu as pltpu
from jax.sharding import PartitionSpec as P

BLOCK = 256
MOST = 8
REACH = 4
CHUNK = 128
HALF = 64
NEG = -1e30
F32 = jnp.float32
MESH = pl.DeviceIdType.MESH

X_IN = (
    (40, 34, 41, 35, 36, 37, 38, 39, 32, 33, 10, 11),
    (38, 44, 39, 45, 43, 42, 14, 15, 33, 32, 37, 36),
)
Y_IN = (
    (20, 30, 21, 31, 22, 28, 23, 29, 12, 13, 14, 15),
    (27, 16, 26, 25, 24, 40, 41, 17, 18, 19, 34, 35),
)
Z_IN = (
    (8, 2, 9, 3, 4, 5, 6, 7),
    (6, 12, 7, 13, 11, 8, 10, 9),
)
BACK = ((17, 16), (21, 20))
OWN = (((16, 17, 18, 19), (24, 25, 26, 27)), ((20, 21, 22, 23), (28, 29, 30, 31)))
STEPS = 13


def pairs_of(t, k):
    low = 8 * k + 4 * t + 2
    ready = [[] for _ in range(STEPS)]
    for s in OWN[t][1 - k]:
        ready[0].append(s)
    for i in range(12):
        for s in (X_IN[t][i], Y_IN[t][i]):
            ready[i + 1].append(s)
    for i in range(8):
        ready[i // 2 * 2 + 4].append(Z_IN[t][i])
    pool, out = [], []
    for u in range(STEPS):
        pool += [s for s in ready[u] if low <= s < low + 32]
        now = []
        while len(pool) >= 2 and len(now) < 2:
            now.append((pool.pop(0), pool.pop(0)))
        out.append(now)
    assert not pool and sum(map(len, out)) == 14
    return out


def events_of(t):
    x_out = [("T", s - (14 if t == 0 else 10)) if s < 16 else ("S", 63 - s) for s in X_IN[1 - t]]
    y_out = [("S", s) for s in Y_IN[1 - t]]
    z_out = [("S", s + 32) for s in Z_IN[t]]
    lists = {"X": x_out, "Y": y_out, "Z": z_out}
    ahead = {"X": 0, "Y": 0, "Z": 0}
    have = {("S", s) for c in range(2) for s in OWN[t][c]}

    def ready():
        out = []
        for link, items in lists.items():
            while ahead[link] < len(items) and items[ahead[link]] in have:
                out.append((link, ahead[link]))
                ahead[link] += 1
        return out

    first = ready()
    steps = []
    for u in range(STEPS):
        now = []
        if u < 12:
            now += [("X", u, ("S", X_IN[t][u])), ("Y", u, ("S", Y_IN[t][u]))]
        if u == 1:
            now.append(("T", 0, ("T", 0), ("T", 1)))
        if u in (3, 5, 7, 9):
            now.append(("Z", (u - 3) // 2, *[("S", s) for s in Z_IN[t][u - 3:u - 1]]))
        done = []
        for kind, i, *items in now:
            have.update(items)
            done.append((kind, i, ready()))
        steps.append(done)
    assert all(ahead[link] == len(items) for link, items in lists.items())
    return lists, first, steps


def kernel(
    row_axis, col_axis, devices, cols, scale,
    cluster_hbm, e_hbm, shift_hbm,
    grad_ref, loss_ref,
    buf, thru, scores, first_exp, weights, top, total, lse_col, lse_send, lse_far, pos_score, qcol_ref, qrow_ref,
    cluster_ref, shift_ref,
    rx, ry, rz, rt, rc, ro, sent, ls, lr, own_sem,
):
    me = lax.axis_index(row_axis) * cols + lax.axis_index(col_axis)
    y = me % 2
    c = me // 2 % 2
    x = me // 4 % 2
    g = 2 * c + y
    yt = (x + y) % 2
    ct = (x + c) % 2
    xpeer = me + 4 - 8 * x
    ypeer = me + 1 - 2 * y
    cpeer = me + 2 - 4 * c
    zto = me + 8 - 16 * x
    zfrom = me - 8 + 16 * x
    z_send = (zto >= 0) & (zto < devices)
    z_recv = (zfrom >= 0) & (zfrom < devices)

    def at(device):
        return (device // cols, device % cols)

    def exists(device):
        return (device >= 0) & (device < devices)

    def when(cond, action):
        if cond is True:
            action()
        else:
            pl.when(cond)(action)

    def both(*conds):
        conds = [cond for cond in conds if cond is not True]
        return functools.reduce(lambda a, b: a & b, conds) if conds else True

    barrier = pltpu.get_barrier_semaphore()
    count = jnp.int32(0)
    for there, device in ((True, xpeer), (True, ypeer), (True, cpeer), (z_send, zto), (z_recv, zfrom)):
        when(there, lambda: pl.semaphore_signal(barrier, inc=1, device_id=at(device), device_id_type=MESH))
        count = count + (1 if there is True else there.astype(jnp.int32))
    pl.semaphore_wait(barrier, count)

    n = e_hbm.shape[0] * CHUNK
    first = 16 + 4 * g

    def slot_of(s):
        return s + x * (47 - 2 * s)

    def rows(slot, half):
        return buf.at[slot, pl.ds(pl.multiple_of(half * HALF, HALF), HALF), :]

    def copy(src, dst, send, receive, device):
        return pltpu.make_async_remote_copy(
            src_ref=src, dst_ref=dst, send_sem=send, recv_sem=receive,
            device_id=at(device), device_id_type=MESH,
        )

    def some(count):
        return buf.at[pl.ds(0, count), pl.ds(0, HALF), :]

    def got(sem, count):
        copy(some(count), some(count), sent.at[0], sem, cpeer).wait_recv()

    def gone(sem, count):
        if count:
            copy(some(count), some(count), sem, rt.at[0], cpeer).wait_send()

    def mine(s, half):
        return e_hbm.at[slot_of(s) - first, pl.ds(pl.multiple_of(half * HALF, HALF), HALF), :]

    def source(item, own):
        kind, s = item
        if kind == "T":
            return thru.at[pl.ds(s * HALF, HALF), :]
        return mine(s, c) if own else rows(slot_of(s), c)

    def link_cond(t, link, i):
        if link in "BZ":
            return "R" if link == "B" else "S"
        if link == "X":
            return "S" if X_IN[1 - t][i] < 16 else True
        return "R" if Y_IN[1 - t][i] < 16 else True

    def holds(cond):
        return {"S": z_send, "R": z_recv, True: True}[cond]

    def link_send(t, lists, link, i, own=False):
        cond = link_cond(t, link, i)
        sem = sent.at[{True: 0, "S": 1, "R": 2}[cond]]
        if link == "B":
            todo = copy(source(("S", BACK[t][i]), own), thru.at[pl.ds(i * HALF, HALF), :], sem, rt.at[0], zfrom)
        elif link == "X":
            s = X_IN[1 - t][i]
            todo = copy(source(lists[link][i], own), rows(s + (1 - x) * (47 - 2 * s), c), sem, rx.at[i], xpeer)
        elif link == "Y":
            todo = copy(source(lists[link][i], own), rows(slot_of(Y_IN[1 - t][i]), c), sem, ry.at[i], ypeer)
        else:
            todo = copy(source(lists[link][i], own), rows(slot_of(Z_IN[t][i]), c), sem, rz.at[i // 2], zto)
        when(holds(cond), lambda: todo.start())

    pairs = [[pairs_of(t, k) for k in range(2)] for t in range(2)]

    def pair_of(t, k, s):
        return [s in pair for now in pairs[t][k] for pair in now].index(True)

    def c_need(t, s):
        return [k for k in range(2) if 8 * (1 - k) + 4 * t + 2 <= s <= 8 * (1 - k) + 4 * t + 33]

    def c_send(t, s):
        for k in c_need(t, s):
            sem = sent.at[2 if s < 16 else 3]
            spot = rows(slot_of(s), c)
            when(both(ct == k, z_recv if s < 16 else True), lambda: copy(
                spot, spot, sem, rc.at[pair_of(t, 1 - k, s)], cpeer).start())

    plans = [events_of(t) for t in range(2)]

    own_copy = pltpu.make_async_copy(e_hbm, buf.at[pl.ds(first, 4)], own_sem.at[2])
    cluster_copy = pltpu.make_async_copy(cluster_hbm, cluster_ref, own_sem.at[0])
    shift_copy = pltpu.make_async_copy(shift_hbm, shift_ref, own_sem.at[1])
    for t in range(2):
        for k in range(2):
            @pl.when((yt == t) & (ct == k))
            def _():
                lists, first, _ = plans[t]
                opening = [(link, i) for link, i in first] + [("B", i) for i in range(2)]

                def slot_at(link, i):
                    return BACK[t][i] if link == "B" else lists[link][i][1]

                def send(link, i, own):
                    link_send(t, lists, link, i, own)

                queue = {link: [i for name, i in opening if name == link] for link in ("X", "Y", "B")}
                plan = {}
                for link, items in queue.items():
                    mine_, other = ([i for i in items if (slot_at(link, i) in OWN[t][k]) == flag] for flag in (True, False))
                    order = []
                    for spot in range(len(items)):
                        take = mine_ if (spot == 0 and mine_) or not other or (mine_ and mine_[0] < other[0]) else other
                        order.append(take.pop(0))
                    plan[link] = order
                leads = []
                for link in ("Y", "X", "B"):
                    while plan[link] and slot_at(link, plan[link][0]) in OWN[t][k]:
                        leads.append((link, plan[link].pop(0)))
                for link, i in leads[:2]:
                    send(link, i, True)
                uses = []
                for link in ("Y", "X", "B", "Y", "X", "B", "Y", "X", "B", "Y", "X", "B", "Y", "Y", "Y", "Y", "X", "X"):
                    if plan[link]:
                        uses.append((link, plan[link].pop(0)))
                assert not any(plan.values())
                order = []
                for s in [s for link, i in [*leads, *uses] for s in [slot_at(link, i)]] + list(OWN[t][k]):
                    if s in OWN[t][k] and s not in order:
                        order.append(s)
                for s in order:
                    copy(
                        mine(s, 1 - c), rows(slot_of(s), 1 - c), sent.at[3], ro.at[OWN[t][k].index(s)],
                        cpeer).start()
                for link, i in leads[2:]:
                    send(link, i, True)
                own_copy.start()
                cluster_copy.start()
                shift_copy.start()
                for s in order:
                    copy(
                        mine(s, c), rows(slot_of(s), c), sent.at[3], rc.at[pair_of(t, 1 - k, s)], cpeer).start()
                waited = set()
                for link, i in uses:
                    s = slot_at(link, i)
                    if s in OWN[t][k]:
                        send(link, i, True)
                        continue
                    if s not in waited:
                        waited.add(s)
                        got(ro.at[OWN[t][1 - k].index(s)], 1)
                    send(link, i, False)
                for s in OWN[t][1 - k]:
                    if s not in waited:
                        got(ro.at[OWN[t][1 - k].index(s)], 1)

    adj = 32 * x
    when(~z_recv, lambda: buf.__setitem__(
        pl.ds(adj, 16), jnp.zeros((16, *buf.shape[1:]), buf.dtype)))
    for offset in (-4, -3, -2, -1, 1, 2, 3, 4):
        when(~exists(me + offset), lambda: lse_far.__setitem__(
            pl.ds(2 * (offset + REACH), 2), jnp.zeros((2, *lse_far.shape[1:]), F32)))

    blocks = cluster_ref.shape[0]
    cluster_copy.wait()
    shift_copy.wait()

    def alive(k, r):
        there = 2 * me + k - 7
        near = jnp.maximum(jnp.minimum(there, blocks - 1), 0)
        same = cluster_ref[near] == cluster_ref[2 * me + r]
        return same & (there == near)

    place = lax.broadcasted_iota(jnp.int32, (1, n), 1)
    within = place % BLOCK
    goal = place - within + (within + shift_ref[...]) % BLOCK
    qrow_ref[...] = goal
    qcol_ref[...] = jnp.broadcast_to(goal.astype(F32), (128, n)).T[:, :1].astype(jnp.int32)

    own_copy.wait()
    half = lax.broadcasted_iota(jnp.int32, (n, BLOCK), 0)
    lane = lax.broadcasted_iota(jnp.int32, (n, BLOCK), 1)
    q = qcol_ref[...]
    own_scores = []
    for h in range(2):
        s = lax.dot_general(
            buf[pl.ds(first, 4)].reshape(n, -1), buf[pl.ds(first + 2 * h, 2)].reshape(BLOCK, -1), (((1,), (1,)), ((), ())),
            preferred_element_type=F32) * scale
        cell = lane + h * BLOCK
        hit = jnp.sum(jnp.where(q == cell, s, 0.0), axis=1, keepdims=True)
        own_scores.append(hit)
        ok = jnp.concatenate(
            [jnp.full((BLOCK, BLOCK), alive(7 + h, r).astype(jnp.int32), jnp.int32) for r in range(2)], 0) > 0
        s = jnp.where(ok & (half != cell), s, NEG)
        for i in range(2):
            scores[14 + 2 * h + i] = s[:, i * CHUNK:(i + 1) * CHUNK]
    pos_score[...] = own_scores[0] + own_scores[1]
    near = [scores[14 + i] for i in range(4)]
    m = functools.reduce(jnp.maximum, near)
    top[...] = m
    total[...] = functools.reduce(jnp.add, [jnp.exp(s - m) for s in near])

    def process(slots):
        ks = [slot // 2 - (2 * g + 1) for slot in slots]

        @pl.when(slots[0] >= 0)
        def _():
            far = jnp.concatenate([buf[slot] for slot in slots], 0)
            s = lax.dot_general(
                buf[pl.ds(first, 4)].reshape(n, -1), far,
                (((1,), (1,)), ((), ())), preferred_element_type=F32) * scale
            for r in range(2):
                part = slice(r * BLOCK, (r + 1) * BLOCK)
                halves = [
                    jnp.where(alive(k, r), s[part, i * CHUNK:(i + 1) * CHUNK], NEG) for i, k in enumerate(ks)]
                for slot, value in zip(slots, halves):
                    scores[slot - (4 * g + 2), part, :] = value
                old = top[part, :]
                new = jnp.maximum(old, jnp.maximum(*halves))
                total[part, :] = total[part, :] * jnp.exp(old - new) + (
                    jnp.exp(halves[0] - new) + jnp.exp(halves[1] - new))
                top[part, :] = new

    def event(t, kind, i, sends):
        lists = plans[t][0]
        if kind == "T":
            when(z_send, lambda: got(rt.at[0], 2))
            slots = []
        elif kind == "Z":
            when(z_recv, lambda: got(rz.at[i], 2))
            slots = Z_IN[t][2 * i:2 * i + 2]
        else:
            slots = [{"X": X_IN, "Y": Y_IN}[kind][t][i]]
            sem = {"X": rx, "Y": ry}[kind].at[i]
            when(z_recv if slots[0] < 16 else True, lambda: got(sem, 1))
        for link, j in sends:
            link_send(t, lists, link, j)
        for s in slots:
            c_send(t, s)

    def c_wait(t, k, pair):
        sem = rc.at[pair_of(t, k, pair[0])]
        count = sum(s >= 16 for s in pair)
        if count == 2:
            got(sem, 2)
            return
        when(z_recv, lambda: got(sem, 2))
        if count:
            when(~z_recv, lambda: got(sem, 1))

    for u in range(STEPS):
        for t in range(2):
            @pl.when(yt == t)
            def _():
                for kind, i, sends in plans[t][2][u]:
                    event(t, kind, i, sends)
                for k in range(2):
                    now = pairs[t][k][u]
                    if now:
                        @pl.when(ct == k)
                        def _():
                            for pair in now:
                                c_wait(t, k, pair)
        for h in range(max(len(pairs[t][k][u]) for t in range(2) for k in range(2))):
            spots = [jnp.int32(-1), jnp.int32(-1)]
            for t in range(2):
                for k in range(2):
                    if h < len(pairs[t][k][u]):
                        here = (yt == t) & (ct == k)
                        spots = [jnp.where(here, slot_of(s), spot) for s, spot in zip(pairs[t][k][u][h], spots)]
            process(spots)

    eye = lax.broadcasted_iota(jnp.int32, (CHUNK, CHUNK), 0) == lax.broadcasted_iota(jnp.int32, (CHUNK, CHUNK), 1)

    def as_row(column):
        return jnp.sum(jnp.where(eye, jnp.broadcast_to(column, (CHUNK, CHUNK)), 0.0), axis=0, keepdims=True)

    lse_rows = []
    for i in range(n // CHUNK):
        part = slice(i * CHUNK, (i + 1) * CHUNK)
        m = jnp.max(top[part, :], axis=1, keepdims=True)
        t = jnp.sum(total[part, :] * jnp.exp(top[part, :] - m), axis=1, keepdims=True)
        lse_rows.append(as_row(m) + jnp.log(as_row(t)))
        lse_col[part, :] = m + jnp.log(t)
    for h in range(2):
        row = jnp.concatenate(lse_rows[2 * h:2 * h + 2], 1)
        lse_send[h] = row
        lse_far[2 * REACH + h] = row

    def lse_copy(offset):
        return copy(
            lse_send, lse_far.at[pl.ds(2 * (REACH - offset), 2)], ls.at[0], lr.at[0], me + offset)

    for offset in (-4, 4, -3, 3, -2, 2, -1, 1):
        when(exists(me + offset), lambda: lse_copy(offset).start())

    loss_ref[...] = jnp.concatenate([row - as_row(pos_score[i * CHUNK:(i + 1) * CHUNK, :]) for i, row in enumerate(lse_rows)], 1)[0]

    lows = []
    for r in range(2):
        low = jnp.int32(r)
        for k in range(r, 7 + r):
            low = low + jnp.where(alive(k, r), 0, 1)
        lows.append(low)

    for h in range(2):
        s = jnp.concatenate([scores[14 + 2 * h + i] for i in range(2)], 1)
        w = jnp.exp(s - lse_col[...]) + jnp.exp(s - lse_far[2 * REACH + h])
        cell = lax.broadcasted_iota(jnp.int32, (n, BLOCK), 1) + h * BLOCK
        line = lax.broadcasted_iota(jnp.int32, (n, BLOCK), 0)
        w = w - (qcol_ref[...] == cell).astype(F32)
        w = w - (qrow_ref[0:1, h * BLOCK:(h + 1) * BLOCK] == line).astype(F32)
        weights[:, h * BLOCK:(h + 1) * BLOCK] = w.astype(jnp.bfloat16)
        for i in range(2):
            scores[14 + 2 * h + i] = jnp.full((n, CHUNK), NEG, F32)

    width = e_hbm.shape[2]

    def own_product(t, carry):
        columns = pl.ds(pl.multiple_of(t * 256, 256), 256)
        grad_ref[:, columns] = jnp.dot(
            weights[:, :2 * BLOCK], buf[pl.ds(first, 4), :, columns].reshape(n, -1), preferred_element_type=F32)
        return carry

    lax.fori_loop(0, width // 256, own_product, 0)

    for r in range(2):
        part = pl.ds(r * BLOCK, BLOCK)
        for j in range(2 * MOST):
            first_exp[part, j * CHUNK:(j + 1) * CHUNK] = jnp.exp(scores[2 * lows[r] + j, part, :] - lse_col[part, :])

    partners = jnp.minimum(me, REACH) + jnp.minimum(devices - 1 - me, REACH)

    def lse_all(count):
        spot = lse_far.at[pl.ds(0, 2 * count)]
        return copy(spot, spot, ls.at[0], lr.at[0], cpeer)

    for count in range(REACH, 2 * REACH + 1):
        when(partners == count, lambda: lse_all(count).wait_recv())
    for r in range(2):
        part = pl.ds(r * BLOCK, BLOCK)
        for j in range(MOST):
            far = lse_far[lows[r] + j + 1]
            for i in range(2):
                spot = slice((2 * j + i) * CHUNK, (2 * j + i + 1) * CHUNK)
                w = first_exp[part, spot] + jnp.exp(
                    scores[2 * lows[r] + 2 * j + i, part, :] - far[:, i * CHUNK:(i + 1) * CHUNK])
                weights[part, spot] = w.astype(jnp.bfloat16)

    for t in range(width // 256):
        columns = pl.ds(t * 256, 256)
        for r in range(2):
            part = pl.ds(r * BLOCK, BLOCK)
            near = jnp.concatenate([buf[4 * g + 2 + 2 * lows[r] + j, :, columns] for j in range(2 * MOST)], 0)
            rest = jnp.dot(weights[part, :], near, preferred_element_type=F32)
            grad_ref[part, columns] = (grad_ref[part, columns] + rest) * scale

    for count in range(REACH, 2 * REACH + 1):
        when(partners == count, lambda: lse_all(count).wait_send())
    for t in range(2):
        conds = [link_cond(t, link, i) for link, items in plans[t][0].items() for i in range(len(items))] + ["R", "R"]
        arrivals = [s for steps in (X_IN[t], Y_IN[t], Z_IN[t]) for s in steps]
        for k in range(2):
            @pl.when((yt == t) & (ct == k))
            def _():
                relayed = [s for s in arrivals if k in c_need(t, s)]
                gone(sent.at[0], conds.count(True))
                when(z_send, lambda: gone(sent.at[1], conds.count("S")))
                when(z_recv, lambda: gone(sent.at[2], conds.count("R") + sum(s < 16 for s in relayed)))
                gone(sent.at[3], 8 + sum(s >= 16 for s in relayed))


def store(grad_ref, loss_ref, grad_out, loss_out, sem):
    parts = 4
    rows = grad_ref.shape[0] // parts
    copies = [pltpu.make_async_copy(loss_ref, loss_out, sem.at[parts])]
    for i in range(parts):
        spot = (pl.ds(i * rows, rows), slice(None))
        copies.append(pltpu.make_async_copy(grad_ref.at[spot], grad_out.at[spot], sem.at[i]))
    for todo in copies:
        todo.start()
    for todo in copies:
        todo.wait()


def solution(mesh):
    row_axis, col_axis = mesh.axis_names
    devices = mesh.shape[row_axis] * mesh.shape[col_axis]
    cols = mesh.shape[col_axis]

    def shards(embeddings, block_cluster, partner_shift):
        rows, width = embeddings.shape
        vmem = pl.BlockSpec(memory_space=pltpu.VMEM)
        hbm = pl.BlockSpec(memory_space=pl.ANY)
        grad, loss = pl.pallas_call(
            functools.partial(kernel, row_axis, col_axis, devices, cols, width ** (-0.5)),
            out_shape=(
                jax.ShapeDtypeStruct((rows, width), F32),
                jax.ShapeDtypeStruct((rows,), F32),
            ),
            in_specs=[hbm, hbm, hbm],
            out_specs=(vmem, vmem),
            scratch_shapes=[
                pltpu.VMEM((48, CHUNK, width), jnp.bfloat16),
                pltpu.VMEM((2 * HALF, width), jnp.bfloat16),
                pltpu.VMEM((32, rows, CHUNK), F32),
                pltpu.VMEM((rows, MOST * BLOCK), F32),
                pltpu.VMEM((rows, MOST * BLOCK), jnp.bfloat16),
                pltpu.VMEM((rows, CHUNK), F32),
                pltpu.VMEM((rows, CHUNK), F32),
                pltpu.VMEM((rows, 1), F32),
                pltpu.VMEM((2, 1, BLOCK), F32),
                pltpu.VMEM((2 * (2 * REACH + 1), 1, BLOCK), F32),
                pltpu.VMEM((rows, 1), F32),
                pltpu.VMEM((rows, 1), jnp.int32),
                pltpu.VMEM((1, rows), jnp.int32),
                pltpu.SMEM(block_cluster.shape, jnp.int32),
                pltpu.VMEM((1, rows), jnp.int32),
                pltpu.SemaphoreType.DMA((12,)),
                pltpu.SemaphoreType.DMA((12,)),
                pltpu.SemaphoreType.DMA((4,)),
                pltpu.SemaphoreType.DMA((1,)),
                pltpu.SemaphoreType.DMA((14,)),
                pltpu.SemaphoreType.DMA((4,)),
                pltpu.SemaphoreType.DMA((4,)),
                pltpu.SemaphoreType.DMA((1,)),
                pltpu.SemaphoreType.DMA((1,)),
                pltpu.SemaphoreType.DMA((3,)),
            ],
            compiler_params=pltpu.CompilerParams(
                collective_id=0, has_side_effects=True, vmem_limit_bytes=36 * 1024 * 1024
            ),
        )(*[pltpu.with_memory_space_constraint(a, pltpu.HBM) for a in (
            block_cluster, embeddings.reshape(rows // CHUNK, CHUNK, width), partner_shift.reshape(1, rows))])
        grad, loss = pl.pallas_call(
            store,
            out_shape=(jax.ShapeDtypeStruct(grad.shape, F32), jax.ShapeDtypeStruct(loss.shape, F32)),
            in_specs=[vmem, vmem],
            out_specs=(hbm, hbm),
            scratch_shapes=[pltpu.SemaphoreType.DMA((5,))],
            compiler_params=pltpu.CompilerParams(vmem_limit_bytes=36 * 1024 * 1024),
        )(grad, loss)
        return loss, grad

    in_specs = (P((row_axis, col_axis), None), P(), P((row_axis, col_axis)))
    out_specs = (P((row_axis, col_axis)), P((row_axis, col_axis), None))
    return jax.shard_map(shards, mesh=mesh, in_specs=in_specs, out_specs=out_specs, check_vma=False)
```

```python
import functools

import jax
import jax.numpy as jnp
from jax import lax
from jax.experimental import pallas as pl
from jax.experimental.pallas import tpu as pltpu
from jax.sharding import PartitionSpec as P

BLOCK = 256
MOST = 8
REACH = 4
CHUNK = 128
HALF = 64
NEG = -1e30
F32 = jnp.float32
MESH = pl.DeviceIdType.MESH

X_IN = (
    (40, 34, 41, 35, 36, 37, 38, 39, 32, 33, 10, 11),
    (38, 44, 39, 45, 43, 42, 14, 15, 33, 32, 37, 36),
)
Y_IN = (
    (20, 30, 21, 31, 22, 28, 23, 29, 12, 13, 14, 15),
    (27, 16, 26, 25, 24, 40, 41, 17, 18, 19, 34, 35),
)
Z_IN = (
    (8, 2, 9, 3, 4, 5, 6, 7),
    (6, 12, 7, 13, 11, 8, 10, 9),
)
BACK = ((17, 16), (21, 20))
OWN = (((16, 17, 18, 19), (24, 25, 26, 27)), ((20, 21, 22, 23), (28, 29, 30, 31)))
STEPS = 13


def pairs_of(t, k):
    low = 8 * k + 4 * t + 2
    ready = [[] for _ in range(STEPS)]
    for s in OWN[t][1 - k]:
        ready[0].append(s)
    for i in range(12):
        for s in (X_IN[t][i], Y_IN[t][i]):
            ready[i + 1].append(s)
    for i in range(8):
        ready[i // 2 * 2 + 4].append(Z_IN[t][i])
    pool, out = [], []
    for u in range(STEPS):
        pool += [s for s in ready[u] if low <= s < low + 32]
        now = []
        while len(pool) >= 2 and len(now) < 2:
            now.append((pool.pop(0), pool.pop(0)))
        out.append(now)
    assert not pool and sum(map(len, out)) == 14
    return out


def events_of(t):
    x_out = [("T", s - (14 if t == 0 else 10)) if s < 16 else ("S", 63 - s) for s in X_IN[1 - t]]
    y_out = [("S", s) for s in Y_IN[1 - t]]
    z_out = [("S", s + 32) for s in Z_IN[t]]
    lists = {"X": x_out, "Y": y_out, "Z": z_out}
    ahead = {"X": 0, "Y": 0, "Z": 0}
    have = {("S", s) for c in range(2) for s in OWN[t][c]}

    def ready():
        out = []
        for link, items in lists.items():
            while ahead[link] < len(items) and items[ahead[link]] in have:
                out.append((link, ahead[link]))
                ahead[link] += 1
        return out

    first = ready()
    steps = []
    for u in range(STEPS):
        now = []
        if u < 12:
            now += [("X", u, ("S", X_IN[t][u])), ("Y", u, ("S", Y_IN[t][u]))]
        if u == 1:
            now.append(("T", 0, ("T", 0), ("T", 1)))
        if u in (3, 5, 7, 9):
            now.append(("Z", (u - 3) // 2, *[("S", s) for s in Z_IN[t][u - 3:u - 1]]))
        done = []
        for kind, i, *items in now:
            have.update(items)
            done.append((kind, i, ready()))
        steps.append(done)
    assert all(ahead[link] == len(items) for link, items in lists.items())
    return lists, first, steps


def kernel(
    row_axis, col_axis, devices, cols, scale,
    cluster_hbm, e_hbm, shift_hbm,
    grad_ref, loss_ref,
    buf, thru, scores, first_exp, weights, top, total, lse_col, lse_send, lse_far, pos_score, qcol_ref, qrow_ref,
    cluster_ref, shift_ref,
    rx, ry, rz, rt, rc, ro, sent, ls, lr, own_sem,
):
    me = lax.axis_index(row_axis) * cols + lax.axis_index(col_axis)
    y = me % 2
    c = me // 2 % 2
    x = me // 4 % 2
    g = 2 * c + y
    yt = (x + y) % 2
    ct = (x + c) % 2
    xpeer = me + 4 - 8 * x
    ypeer = me + 1 - 2 * y
    cpeer = me + 2 - 4 * c
    zto = me + 8 - 16 * x
    zfrom = me - 8 + 16 * x
    z_send = (zto >= 0) & (zto < devices)
    z_recv = (zfrom >= 0) & (zfrom < devices)

    def at(device):
        return (device // cols, device % cols)

    def exists(device):
        return (device >= 0) & (device < devices)

    def when(cond, action):
        if cond is True:
            action()
        else:
            pl.when(cond)(action)

    def both(*conds):
        conds = [cond for cond in conds if cond is not True]
        return functools.reduce(lambda a, b: a & b, conds) if conds else True

    barrier = pltpu.get_barrier_semaphore()
    count = jnp.int32(0)
    for there, device in ((True, xpeer), (True, ypeer), (True, cpeer), (z_send, zto), (z_recv, zfrom)):
        when(there, lambda: pl.semaphore_signal(barrier, inc=1, device_id=at(device), device_id_type=MESH))
        count = count + (1 if there is True else there.astype(jnp.int32))
    pl.semaphore_wait(barrier, count)

    n = e_hbm.shape[0] * CHUNK
    first = 16 + 4 * g

    def slot_of(s):
        return s + x * (47 - 2 * s)

    def rows(slot, half):
        return buf.at[slot, pl.ds(pl.multiple_of(half * HALF, HALF), HALF), :]

    def copy(src, dst, send, receive, device):
        return pltpu.make_async_remote_copy(
            src_ref=src, dst_ref=dst, send_sem=send, recv_sem=receive,
            device_id=at(device), device_id_type=MESH,
        )

    def some(count):
        return buf.at[pl.ds(0, count), pl.ds(0, HALF), :]

    def got(sem, count):
        copy(some(count), some(count), sent.at[0], sem, cpeer).wait_recv()

    def gone(sem, count):
        if count:
            copy(some(count), some(count), sem, rt.at[0], cpeer).wait_send()

    def mine(s, half):
        return e_hbm.at[slot_of(s) - first, pl.ds(pl.multiple_of(half * HALF, HALF), HALF), :]

    def source(item, own):
        kind, s = item
        if kind == "T":
            return thru.at[pl.ds(s * HALF, HALF), :]
        return mine(s, c) if own else rows(slot_of(s), c)

    def link_cond(t, link, i):
        if link in "BZ":
            return "R" if link == "B" else "S"
        if link == "X":
            return "S" if X_IN[1 - t][i] < 16 else True
        return "R" if Y_IN[1 - t][i] < 16 else True

    def holds(cond):
        return {"S": z_send, "R": z_recv, True: True}[cond]

    def link_send(t, lists, link, i, own=False):
        cond = link_cond(t, link, i)
        sem = sent.at[{True: 0, "S": 1, "R": 2}[cond]]
        if link == "B":
            todo = copy(source(("S", BACK[t][i]), own), thru.at[pl.ds(i * HALF, HALF), :], sem, rt.at[0], zfrom)
        elif link == "X":
            s = X_IN[1 - t][i]
            todo = copy(source(lists[link][i], own), rows(s + (1 - x) * (47 - 2 * s), c), sem, rx.at[i], xpeer)
        elif link == "Y":
            todo = copy(source(lists[link][i], own), rows(slot_of(Y_IN[1 - t][i]), c), sem, ry.at[i], ypeer)
        else:
            todo = copy(source(lists[link][i], own), rows(slot_of(Z_IN[t][i]), c), sem, rz.at[i // 2], zto)
        when(holds(cond), lambda: todo.start())

    pairs = [[pairs_of(t, k) for k in range(2)] for t in range(2)]

    def pair_of(t, k, s):
        return [s in pair for now in pairs[t][k] for pair in now].index(True)

    def c_need(t, s):
        return [k for k in range(2) if 8 * (1 - k) + 4 * t + 2 <= s <= 8 * (1 - k) + 4 * t + 33]

    def c_send(t, s):
        for k in c_need(t, s):
            sem = sent.at[2 if s < 16 else 3]
            spot = rows(slot_of(s), c)
            when(both(ct == k, z_recv if s < 16 else True), lambda: copy(
                spot, spot, sem, rc.at[pair_of(t, 1 - k, s)], cpeer).start())

    plans = [events_of(t) for t in range(2)]

    own_copy = pltpu.make_async_copy(e_hbm, buf.at[pl.ds(first, 4)], own_sem.at[2])
    cluster_copy = pltpu.make_async_copy(cluster_hbm, cluster_ref, own_sem.at[0])
    shift_copy = pltpu.make_async_copy(shift_hbm, shift_ref, own_sem.at[1])
    for t in range(2):
        for k in range(2):
            @pl.when((yt == t) & (ct == k))
            def _():
                lists, first, _ = plans[t]
                opening = [(link, i) for link, i in first] + [("B", i) for i in range(2)]

                def slot_at(link, i):
                    return BACK[t][i] if link == "B" else lists[link][i][1]

                def send(link, i, own):
                    link_send(t, lists, link, i, own)

                queue = {link: [i for name, i in opening if name == link] for link in ("X", "Y", "B")}
                plan = {}
                for link, items in queue.items():
                    mine_, other = ([i for i in items if (slot_at(link, i) in OWN[t][k]) == flag] for flag in (True, False))
                    order = []
                    for spot in range(len(items)):
                        take = mine_ if (spot == 0 and mine_) or not other or (mine_ and mine_[0] < other[0]) else other
                        order.append(take.pop(0))
                    plan[link] = order
                leads = []
                for link in ("Y", "X", "B"):
                    while plan[link] and slot_at(link, plan[link][0]) in OWN[t][k]:
                        leads.append((link, plan[link].pop(0)))
                for link, i in leads[:2]:
                    send(link, i, True)
                uses = []
                for link in ("Y", "X", "B", "Y", "X", "B", "Y", "X", "B", "Y", "X", "B", "Y", "Y", "Y", "Y", "X", "X"):
                    if plan[link]:
                        uses.append((link, plan[link].pop(0)))
                assert not any(plan.values())
                order = []
                for s in [s for link, i in [*leads, *uses] for s in [slot_at(link, i)]] + list(OWN[t][k]):
                    if s in OWN[t][k] and s not in order:
                        order.append(s)
                for s in order:
                    copy(
                        mine(s, 1 - c), rows(slot_of(s), 1 - c), sent.at[3], ro.at[OWN[t][k].index(s)],
                        cpeer).start()
                for link, i in leads[2:]:
                    send(link, i, True)
                own_copy.start()
                cluster_copy.start()
                shift_copy.start()
                for s in order:
                    copy(
                        mine(s, c), rows(slot_of(s), c), sent.at[3], rc.at[pair_of(t, 1 - k, s)], cpeer).start()
                waited = set()
                for link, i in uses:
                    s = slot_at(link, i)
                    if s in OWN[t][k]:
                        send(link, i, True)
                        continue
                    if s not in waited:
                        waited.add(s)
                        got(ro.at[OWN[t][1 - k].index(s)], 1)
                    send(link, i, False)
                for s in OWN[t][1 - k]:
                    if s not in waited:
                        got(ro.at[OWN[t][1 - k].index(s)], 1)

    adj = 32 * x
    when(~z_recv, lambda: buf.__setitem__(
        pl.ds(adj, 16), jnp.zeros((16, *buf.shape[1:]), buf.dtype)))
    for offset in (-4, -3, -2, -1, 1, 2, 3, 4):
        when(~exists(me + offset), lambda: lse_far.__setitem__(
            pl.ds(2 * (offset + REACH), 2), jnp.zeros((2, *lse_far.shape[1:]), F32)))

    blocks = cluster_ref.shape[0]
    cluster_copy.wait()
    shift_copy.wait()

    def alive(k, r):
        there = 2 * me + k - 7
        near = jnp.maximum(jnp.minimum(there, blocks - 1), 0)
        same = cluster_ref[near] == cluster_ref[2 * me + r]
        return same & (there == near)

    place = lax.broadcasted_iota(jnp.int32, (1, n), 1)
    within = place % BLOCK
    goal = place - within + (within + shift_ref[...]) % BLOCK
    qrow_ref[...] = goal
    qcol_ref[...] = jnp.broadcast_to(goal.astype(F32), (128, n)).T[:, :1].astype(jnp.int32)

    own_copy.wait()
    half = lax.broadcasted_iota(jnp.int32, (n, BLOCK), 0)
    lane = lax.broadcasted_iota(jnp.int32, (n, BLOCK), 1)
    q = qcol_ref[...]
    own_scores = []
    for h in range(2):
        s = lax.dot_general(
            buf[pl.ds(first, 4)].reshape(n, -1), buf[pl.ds(first + 2 * h, 2)].reshape(BLOCK, -1), (((1,), (1,)), ((), ())),
            preferred_element_type=F32) * scale
        cell = lane + h * BLOCK
        hit = jnp.sum(jnp.where(q == cell, s, 0.0), axis=1, keepdims=True)
        own_scores.append(hit)
        ok = jnp.concatenate(
            [jnp.full((BLOCK, BLOCK), alive(7 + h, r).astype(jnp.int32), jnp.int32) for r in range(2)], 0) > 0
        s = jnp.where(ok & (half != cell), s, NEG)
        for i in range(2):
            scores[14 + 2 * h + i] = s[:, i * CHUNK:(i + 1) * CHUNK]
    pos_score[...] = own_scores[0] + own_scores[1]
    near = [scores[14 + i] for i in range(4)]
    m = functools.reduce(jnp.maximum, near)
    top[...] = m
    total[...] = functools.reduce(jnp.add, [jnp.exp(s - m) for s in near])

    def process(slots):
        ks = [slot // 2 - (2 * g + 1) for slot in slots]

        @pl.when(slots[0] >= 0)
        def _():
            far = jnp.concatenate([buf[slot] for slot in slots], 0)
            s = lax.dot_general(
                buf[pl.ds(first, 4)].reshape(n, -1), far,
                (((1,), (1,)), ((), ())), preferred_element_type=F32) * scale
            for r in range(2):
                part = slice(r * BLOCK, (r + 1) * BLOCK)
                halves = [
                    jnp.where(alive(k, r), s[part, i * CHUNK:(i + 1) * CHUNK], NEG) for i, k in enumerate(ks)]
                for slot, value in zip(slots, halves):
                    scores[slot - (4 * g + 2), part, :] = value
                old = top[part, :]
                new = jnp.maximum(old, jnp.maximum(*halves))
                total[part, :] = total[part, :] * jnp.exp(old - new) + (
                    jnp.exp(halves[0] - new) + jnp.exp(halves[1] - new))
                top[part, :] = new

    def event(t, kind, i, sends):
        lists = plans[t][0]
        if kind == "T":
            when(z_send, lambda: got(rt.at[0], 2))
            slots = []
        elif kind == "Z":
            when(z_recv, lambda: got(rz.at[i], 2))
            slots = Z_IN[t][2 * i:2 * i + 2]
        else:
            slots = [{"X": X_IN, "Y": Y_IN}[kind][t][i]]
            sem = {"X": rx, "Y": ry}[kind].at[i]
            when(z_recv if slots[0] < 16 else True, lambda: got(sem, 1))
        for link, j in sends:
            link_send(t, lists, link, j)
        for s in slots:
            c_send(t, s)

    def c_wait(t, k, pair):
        sem = rc.at[pair_of(t, k, pair[0])]
        count = sum(s >= 16 for s in pair)
        if count == 2:
            got(sem, 2)
            return
        when(z_recv, lambda: got(sem, 2))
        if count:
            when(~z_recv, lambda: got(sem, 1))

    for u in range(STEPS):
        for t in range(2):
            @pl.when(yt == t)
            def _():
                for kind, i, sends in plans[t][2][u]:
                    event(t, kind, i, sends)
                for k in range(2):
                    now = pairs[t][k][u]
                    if now:
                        @pl.when(ct == k)
                        def _():
                            for pair in now:
                                c_wait(t, k, pair)
        for h in range(max(len(pairs[t][k][u]) for t in range(2) for k in range(2))):
            spots = [jnp.int32(-1), jnp.int32(-1)]
            for t in range(2):
                for k in range(2):
                    if h < len(pairs[t][k][u]):
                        here = (yt == t) & (ct == k)
                        spots = [jnp.where(here, slot_of(s), spot) for s, spot in zip(pairs[t][k][u][h], spots)]
            process(spots)

    eye = lax.broadcasted_iota(jnp.int32, (CHUNK, CHUNK), 0) == lax.broadcasted_iota(jnp.int32, (CHUNK, CHUNK), 1)

    def as_row(column):
        return jnp.sum(jnp.where(eye, jnp.broadcast_to(column, (CHUNK, CHUNK)), 0.0), axis=0, keepdims=True)

    lse_rows = []
    for i in range(n // CHUNK):
        part = slice(i * CHUNK, (i + 1) * CHUNK)
        m = jnp.max(top[part, :], axis=1, keepdims=True)
        t = jnp.sum(total[part, :] * jnp.exp(top[part, :] - m), axis=1, keepdims=True)
        lse_rows.append(as_row(m) + jnp.log(as_row(t)))
        lse_col[part, :] = m + jnp.log(t)
    for h in range(2):
        row = jnp.concatenate(lse_rows[2 * h:2 * h + 2], 1)
        lse_send[h] = row
        lse_far[2 * REACH + h] = row

    def lse_copy(offset):
        return copy(
            lse_send, lse_far.at[pl.ds(2 * (REACH - offset), 2)], ls.at[0], lr.at[0], me + offset)

    for offset in (-4, 4, -3, 3, -2, 2, -1, 1):
        when(exists(me + offset), lambda: lse_copy(offset).start())

    loss_ref[...] = jnp.concatenate([row - as_row(pos_score[i * CHUNK:(i + 1) * CHUNK, :]) for i, row in enumerate(lse_rows)], 1)[0]

    lows = []
    for r in range(2):
        low = jnp.int32(r)
        for k in range(r, 7 + r):
            low = low + jnp.where(alive(k, r), 0, 1)
        lows.append(low)

    def live(r, j):
        left = jnp.maximum(7 - lows[r], 0)
        return jnp.where(j < left, lows[r] + j, 9 + j - left)

    for h in range(2):
        s = jnp.concatenate([scores[14 + 2 * h + i] for i in range(2)], 1)
        w = jnp.exp(s - lse_col[...]) + jnp.exp(s - lse_far[2 * REACH + h])
        cell = lax.broadcasted_iota(jnp.int32, (n, BLOCK), 1) + h * BLOCK
        line = lax.broadcasted_iota(jnp.int32, (n, BLOCK), 0)
        w = w - (qcol_ref[...] == cell).astype(F32)
        w = w - (qrow_ref[0:1, h * BLOCK:(h + 1) * BLOCK] == line).astype(F32)
        weights[:, h * BLOCK:(h + 1) * BLOCK] = w.astype(jnp.bfloat16)

    width = e_hbm.shape[2]

    def own_product(t, carry):
        columns = pl.ds(pl.multiple_of(t * 256, 256), 256)
        grad_ref[:, columns] = jnp.dot(
            weights[:, :2 * BLOCK], buf[pl.ds(first, 4), :, columns].reshape(n, -1), preferred_element_type=F32)
        return carry

    lax.fori_loop(0, width // 256, own_product, 0)

    for r in range(2):
        part = pl.ds(r * BLOCK, BLOCK)
        for j in range(MOST - 1):
            for i in range(2):
                spot = slice((2 * j + i) * CHUNK, (2 * j + i + 1) * CHUNK)
                first_exp[part, spot] = jnp.exp(scores[2 * live(r, j) + i, part, :] - lse_col[part, :])

    partners = jnp.minimum(me, REACH) + jnp.minimum(devices - 1 - me, REACH)

    def lse_all(count):
        spot = lse_far.at[pl.ds(0, 2 * count)]
        return copy(spot, spot, ls.at[0], lr.at[0], cpeer)

    for count in range(REACH, 2 * REACH + 1):
        when(partners == count, lambda: lse_all(count).wait_recv())
    for r in range(2):
        part = pl.ds(r * BLOCK, BLOCK)
        for j in range(MOST - 1):
            far = lse_far[live(r, j) + 1]
            for i in range(2):
                spot = slice((2 * j + i) * CHUNK, (2 * j + i + 1) * CHUNK)
                w = first_exp[part, spot] + jnp.exp(
                    scores[2 * live(r, j) + i, part, :] - far[:, i * CHUNK:(i + 1) * CHUNK])
                weights[part, spot] = w.astype(jnp.bfloat16)

    for t in range(width // 256):
        columns = pl.ds(t * 256, 256)
        for r in range(2):
            part = pl.ds(r * BLOCK, BLOCK)
            near = jnp.concatenate(
                [buf[4 * g + 2 + 2 * live(r, j) + i, :, columns] for j in range(MOST - 1) for i in range(2)], 0)
            rest = jnp.dot(weights[part, :], near, preferred_element_type=F32)
            grad_ref[part, columns] = (grad_ref[part, columns] + rest) * scale

    for count in range(REACH, 2 * REACH + 1):
        when(partners == count, lambda: lse_all(count).wait_send())
    for t in range(2):
        conds = [link_cond(t, link, i) for link, items in plans[t][0].items() for i in range(len(items))] + ["R", "R"]
        arrivals = [s for steps in (X_IN[t], Y_IN[t], Z_IN[t]) for s in steps]
        for k in range(2):
            @pl.when((yt == t) & (ct == k))
            def _():
                relayed = [s for s in arrivals if k in c_need(t, s)]
                gone(sent.at[0], conds.count(True))
                when(z_send, lambda: gone(sent.at[1], conds.count("S")))
                when(z_recv, lambda: gone(sent.at[2], conds.count("R") + sum(s < 16 for s in relayed)))
                gone(sent.at[3], 8 + sum(s >= 16 for s in relayed))


def store(grad_ref, loss_ref, grad_out, loss_out, sem):
    parts = 4
    rows = grad_ref.shape[0] // parts
    copies = [pltpu.make_async_copy(loss_ref, loss_out, sem.at[parts])]
    for i in range(parts):
        spot = (pl.ds(i * rows, rows), slice(None))
        copies.append(pltpu.make_async_copy(grad_ref.at[spot], grad_out.at[spot], sem.at[i]))
    for todo in copies:
        todo.start()
    for todo in copies:
        todo.wait()


def solution(mesh):
    row_axis, col_axis = mesh.axis_names
    devices = mesh.shape[row_axis] * mesh.shape[col_axis]
    cols = mesh.shape[col_axis]

    def shards(embeddings, block_cluster, partner_shift):
        rows, width = embeddings.shape
        vmem = pl.BlockSpec(memory_space=pltpu.VMEM)
        hbm = pl.BlockSpec(memory_space=pl.ANY)
        grad, loss = pl.pallas_call(
            functools.partial(kernel, row_axis, col_axis, devices, cols, width ** (-0.5)),
            out_shape=(
                jax.ShapeDtypeStruct((rows, width), F32),
                jax.ShapeDtypeStruct((rows,), F32),
            ),
            in_specs=[hbm, hbm, hbm],
            out_specs=(vmem, vmem),
            scratch_shapes=[
                pltpu.VMEM((48, CHUNK, width), jnp.bfloat16),
                pltpu.VMEM((2 * HALF, width), jnp.bfloat16),
                pltpu.VMEM((32, rows, CHUNK), F32),
                pltpu.VMEM((rows, (MOST - 1) * BLOCK), F32),
                pltpu.VMEM((rows, (MOST - 1) * BLOCK), jnp.bfloat16),
                pltpu.VMEM((rows, CHUNK), F32),
                pltpu.VMEM((rows, CHUNK), F32),
                pltpu.VMEM((rows, 1), F32),
                pltpu.VMEM((2, 1, BLOCK), F32),
                pltpu.VMEM((2 * (2 * REACH + 1), 1, BLOCK), F32),
                pltpu.VMEM((rows, 1), F32),
                pltpu.VMEM((rows, 1), jnp.int32),
                pltpu.VMEM((1, rows), jnp.int32),
                pltpu.SMEM(block_cluster.shape, jnp.int32),
                pltpu.VMEM((1, rows), jnp.int32),
                pltpu.SemaphoreType.DMA((12,)),
                pltpu.SemaphoreType.DMA((12,)),
                pltpu.SemaphoreType.DMA((4,)),
                pltpu.SemaphoreType.DMA((1,)),
                pltpu.SemaphoreType.DMA((14,)),
                pltpu.SemaphoreType.DMA((4,)),
                pltpu.SemaphoreType.DMA((4,)),
                pltpu.SemaphoreType.DMA((1,)),
                pltpu.SemaphoreType.DMA((1,)),
                pltpu.SemaphoreType.DMA((3,)),
            ],
            compiler_params=pltpu.CompilerParams(
                collective_id=0, has_side_effects=True, vmem_limit_bytes=36 * 1024 * 1024
            ),
        )(*[pltpu.with_memory_space_constraint(a, pltpu.HBM) for a in (
            block_cluster, embeddings.reshape(rows // CHUNK, CHUNK, width), partner_shift.reshape(1, rows))])
        grad, loss = pl.pallas_call(
            store,
            out_shape=(jax.ShapeDtypeStruct(grad.shape, F32), jax.ShapeDtypeStruct(loss.shape, F32)),
            in_specs=[vmem, vmem],
            out_specs=(hbm, hbm),
            scratch_shapes=[pltpu.SemaphoreType.DMA((5,))],
            compiler_params=pltpu.CompilerParams(vmem_limit_bytes=36 * 1024 * 1024),
        )(grad, loss)
        return loss, grad

    in_specs = (P((row_axis, col_axis), None), P(), P((row_axis, col_axis)))
    out_specs = (P((row_axis, col_axis)), P((row_axis, col_axis), None))
    return jax.shard_map(shards, mesh=mesh, in_specs=in_specs, out_specs=out_specs, check_vma=False)
```

```python
import functools

import jax
import jax.numpy as jnp
from jax import lax
from jax.experimental import pallas as pl
from jax.experimental.pallas import tpu as pltpu
from jax.sharding import PartitionSpec as P

BLOCK = 256
MOST = 8
REACH = 4
CHUNK = 128
HALF = 64
NEG = -1e30
F32 = jnp.float32
MESH = pl.DeviceIdType.MESH

X_IN = (
    (40, 34, 41, 35, 36, 37, 38, 39, 32, 33, 10, 11),
    (38, 44, 39, 45, 43, 42, 14, 15, 33, 32, 37, 36),
)
Y_IN = (
    (20, 30, 21, 31, 22, 28, 23, 29, 12, 13, 14, 15),
    (27, 16, 26, 25, 24, 40, 41, 17, 18, 19, 34, 35),
)
Z_IN = (
    (8, 2, 9, 3, 4, 5, 6, 7),
    (6, 12, 7, 13, 11, 8, 10, 9),
)
BACK = ((17, 16), (21, 20))
OWN = (((16, 17, 18, 19), (24, 25, 26, 27)), ((20, 21, 22, 23), (28, 29, 30, 31)))
STEPS = 13
LATE = 8


def pairs_of(t, k):
    low = 8 * k + 4 * t + 2
    ready = [[] for _ in range(STEPS)]
    for s in OWN[t][1 - k]:
        ready[0].append(s)
    for i in range(12):
        for s in (X_IN[t][i], Y_IN[t][i]):
            ready[i + 1].append(s)
    for i in range(8):
        ready[i // 2 * 2 + 4].append(Z_IN[t][i])
    pool, out = [], []
    for u in range(STEPS):
        pool += [s for s in ready[u] if low <= s < low + 32]
        now = []
        while len(pool) >= 2 and len(now) < 2:
            now.append((pool.pop(0), pool.pop(0)))
        out.append(now)
    assert not pool and sum(map(len, out)) == 14
    return out


def events_of(t):
    x_out = [("T", s - (14 if t == 0 else 10)) if s < 16 else ("S", 63 - s) for s in X_IN[1 - t]]
    y_out = [("S", s) for s in Y_IN[1 - t]]
    z_out = [("S", s + 32) for s in Z_IN[t]]
    lists = {"X": x_out, "Y": y_out, "Z": z_out}
    ahead = {"X": 0, "Y": 0, "Z": 0}
    have = {("S", s) for c in range(2) for s in OWN[t][c]}

    def ready():
        out = []
        for link, items in lists.items():
            while ahead[link] < len(items) and items[ahead[link]] in have:
                out.append((link, ahead[link]))
                ahead[link] += 1
        return out

    first = ready()
    steps = []
    for u in range(STEPS):
        now = []
        if u < 12:
            now += [("X", u, ("S", X_IN[t][u])), ("Y", u, ("S", Y_IN[t][u]))]
        if u == 1:
            now.append(("T", 0, ("T", 0), ("T", 1)))
        if u in (3, 5, 7, 9):
            now.append(("Z", (u - 3) // 2, *[("S", s) for s in Z_IN[t][u - 3:u - 1]]))
        done = []
        for kind, i, *items in now:
            have.update(items)
            done.append((kind, i, ready()))
        steps.append(done)
    assert all(ahead[link] == len(items) for link, items in lists.items())
    return lists, first, steps


def kernel(
    row_axis, col_axis, devices, cols, scale,
    cluster_hbm, e_hbm, shift_hbm,
    grad_ref, loss_ref,
    buf, thru, scores, first_exp, weights, top, total, lse_col, lse_send, lse_far, pos_score, qcol_ref, qrow_ref,
    cluster_ref, shift_ref,
    rx, ry, rz, rt, rc, ro, sent, ls, lr, own_sem,
):
    me = lax.axis_index(row_axis) * cols + lax.axis_index(col_axis)
    y = me % 2
    c = me // 2 % 2
    x = me // 4 % 2
    g = 2 * c + y
    yt = (x + y) % 2
    ct = (x + c) % 2
    xpeer = me + 4 - 8 * x
    ypeer = me + 1 - 2 * y
    cpeer = me + 2 - 4 * c
    zto = me + 8 - 16 * x
    zfrom = me - 8 + 16 * x
    z_send = (zto >= 0) & (zto < devices)
    z_recv = (zfrom >= 0) & (zfrom < devices)

    def at(device):
        return (device // cols, device % cols)

    def exists(device):
        return (device >= 0) & (device < devices)

    def when(cond, action):
        if cond is True:
            action()
        else:
            pl.when(cond)(action)

    def both(*conds):
        conds = [cond for cond in conds if cond is not True]
        return functools.reduce(lambda a, b: a & b, conds) if conds else True

    barrier = pltpu.get_barrier_semaphore()
    count = jnp.int32(0)
    for there, device in ((True, xpeer), (True, ypeer), (True, cpeer), (z_send, zto), (z_recv, zfrom)):
        when(there, lambda: pl.semaphore_signal(barrier, inc=1, device_id=at(device), device_id_type=MESH))
        count = count + (1 if there is True else there.astype(jnp.int32))
    pl.semaphore_wait(barrier, count)

    n = e_hbm.shape[0] * CHUNK
    first = 16 + 4 * g

    def slot_of(s):
        return s + x * (47 - 2 * s)

    def rows(slot, half):
        return buf.at[slot, pl.ds(pl.multiple_of(half * HALF, HALF), HALF), :]

    def copy(src, dst, send, receive, device):
        return pltpu.make_async_remote_copy(
            src_ref=src, dst_ref=dst, send_sem=send, recv_sem=receive,
            device_id=at(device), device_id_type=MESH,
        )

    def some(count):
        return buf.at[pl.ds(0, count), pl.ds(0, HALF), :]

    def got(sem, count):
        copy(some(count), some(count), sent.at[0], sem, cpeer).wait_recv()

    def gone(sem, count):
        if count:
            copy(some(count), some(count), sem, rt.at[0], cpeer).wait_send()

    def mine(s, half):
        return e_hbm.at[slot_of(s) - first, pl.ds(pl.multiple_of(half * HALF, HALF), HALF), :]

    def source(item, own):
        kind, s = item
        if kind == "T":
            return thru.at[pl.ds(s * HALF, HALF), :]
        return mine(s, c) if own else rows(slot_of(s), c)

    def link_cond(t, link, i):
        if link in "BZ":
            return "R" if link == "B" else "S"
        if link == "X":
            return "S" if X_IN[1 - t][i] < 16 else True
        return "R" if Y_IN[1 - t][i] < 16 else True

    def holds(cond):
        return {"S": z_send, "R": z_recv, True: True}[cond]

    def link_send(t, lists, link, i, own=False):
        cond = link_cond(t, link, i)
        sem = sent.at[{True: 0, "S": 1, "R": 2}[cond]]
        if link == "B":
            todo = copy(source(("S", BACK[t][i]), own), thru.at[pl.ds(i * HALF, HALF), :], sem, rt.at[0], zfrom)
        elif link == "X":
            s = X_IN[1 - t][i]
            todo = copy(source(lists[link][i], own), rows(s + (1 - x) * (47 - 2 * s), c), sem, rx.at[i], xpeer)
        elif link == "Y":
            todo = copy(source(lists[link][i], own), rows(slot_of(Y_IN[1 - t][i]), c), sem, (ry if i < LATE else rx).at[i], ypeer)
        else:
            todo = copy(source(lists[link][i], own), rows(slot_of(Z_IN[t][i]), c), sem, rz.at[i // 2], zto)
        when(holds(cond), lambda: todo.start())

    pairs = [[pairs_of(t, k) for k in range(2)] for t in range(2)]

    def pair_of(t, k, s):
        return [s in pair for now in pairs[t][k] for pair in now].index(True)

    def c_need(t, s):
        return [k for k in range(2) if 8 * (1 - k) + 4 * t + 2 <= s <= 8 * (1 - k) + 4 * t + 33]

    def c_send(t, s):
        for k in c_need(t, s):
            sem = sent.at[2 if s < 16 else 3]
            spot = rows(slot_of(s), c)
            when(both(ct == k, z_recv if s < 16 else True), lambda: copy(
                spot, spot, sem, rc.at[pair_of(t, 1 - k, s)], cpeer).start())

    plans = [events_of(t) for t in range(2)]

    own_copy = pltpu.make_async_copy(e_hbm, buf.at[pl.ds(first, 4)], own_sem.at[2])
    cluster_copy = pltpu.make_async_copy(cluster_hbm, cluster_ref, own_sem.at[0])
    shift_copy = pltpu.make_async_copy(shift_hbm, shift_ref, own_sem.at[1])
    for t in range(2):
        for k in range(2):
            @pl.when((yt == t) & (ct == k))
            def _():
                lists, first, _ = plans[t]
                opening = [(link, i) for link, i in first] + [("B", i) for i in range(2)]

                def slot_at(link, i):
                    return BACK[t][i] if link == "B" else lists[link][i][1]

                def send(link, i, own):
                    link_send(t, lists, link, i, own)

                queue = {link: [i for name, i in opening if name == link] for link in ("X", "Y", "B")}
                plan = {}
                for link, items in queue.items():
                    mine_, other = ([i for i in items if (slot_at(link, i) in OWN[t][k]) == flag] for flag in (True, False))
                    order = []
                    for spot in range(len(items)):
                        take = mine_ if (spot == 0 and mine_) or not other or (mine_ and mine_[0] < other[0]) else other
                        order.append(take.pop(0))
                    plan[link] = order
                leads = []
                for link in ("Y", "X", "B"):
                    while plan[link] and slot_at(link, plan[link][0]) in OWN[t][k]:
                        leads.append((link, plan[link].pop(0)))
                for link, i in leads[:2]:
                    send(link, i, True)
                uses = []
                for link in ("Y", "X", "B", "Y", "X", "B", "Y", "X", "B", "Y", "X", "B", "Y", "Y", "Y", "Y", "X", "X"):
                    if plan[link]:
                        uses.append((link, plan[link].pop(0)))
                assert not any(plan.values())
                order = []
                for s in [s for link, i in [*leads, *uses] for s in [slot_at(link, i)]] + list(OWN[t][k]):
                    if s in OWN[t][k] and s not in order:
                        order.append(s)
                for s in order:
                    copy(
                        mine(s, 1 - c), rows(slot_of(s), 1 - c), sent.at[3], ro.at[OWN[t][k].index(s)],
                        cpeer).start()
                for link, i in leads[2:]:
                    send(link, i, True)
                own_copy.start()
                cluster_copy.start()
                shift_copy.start()
                for s in order:
                    copy(
                        mine(s, c), rows(slot_of(s), c), sent.at[3], rc.at[pair_of(t, 1 - k, s)], cpeer).start()
                waited = set()
                for link, i in uses:
                    s = slot_at(link, i)
                    if s in OWN[t][k]:
                        send(link, i, True)
                        continue
                    if s not in waited:
                        waited.add(s)
                        got(ro.at[OWN[t][1 - k].index(s)], 1)
                    send(link, i, False)
                for s in OWN[t][1 - k]:
                    if s not in waited:
                        got(ro.at[OWN[t][1 - k].index(s)], 1)

    adj = 32 * x
    when(~z_recv, lambda: buf.__setitem__(
        pl.ds(adj, 16), jnp.zeros((16, *buf.shape[1:]), buf.dtype)))
    for offset in (-4, -3, -2, -1, 1, 2, 3, 4):
        when(~exists(me + offset), lambda: lse_far.__setitem__(
            pl.ds(2 * (offset + REACH), 2), jnp.zeros((2, *lse_far.shape[1:]), F32)))

    blocks = cluster_ref.shape[0]
    cluster_copy.wait()
    shift_copy.wait()

    def alive(k, r):
        there = 2 * me + k - 7
        near = jnp.maximum(jnp.minimum(there, blocks - 1), 0)
        same = cluster_ref[near] == cluster_ref[2 * me + r]
        return same & (there == near)

    place = lax.broadcasted_iota(jnp.int32, (1, n), 1)
    within = place % BLOCK
    goal = place - within + (within + shift_ref[...]) % BLOCK
    qrow_ref[...] = goal
    qcol_ref[...] = jnp.broadcast_to(goal.astype(F32), (128, n)).T[:, :1].astype(jnp.int32)

    own_copy.wait()
    half = lax.broadcasted_iota(jnp.int32, (n, BLOCK), 0)
    lane = lax.broadcasted_iota(jnp.int32, (n, BLOCK), 1)
    q = qcol_ref[...]
    own_scores = []
    for h in range(2):
        s = lax.dot_general(
            buf[pl.ds(first, 4)].reshape(n, -1), buf[pl.ds(first + 2 * h, 2)].reshape(BLOCK, -1), (((1,), (1,)), ((), ())),
            preferred_element_type=F32) * scale
        cell = lane + h * BLOCK
        hit = jnp.sum(jnp.where(q == cell, s, 0.0), axis=1, keepdims=True)
        own_scores.append(hit)
        ok = jnp.concatenate(
            [jnp.full((BLOCK, BLOCK), alive(7 + h, r).astype(jnp.int32), jnp.int32) for r in range(2)], 0) > 0
        s = jnp.where(ok & (half != cell), s, NEG)
        for i in range(2):
            scores[14 + 2 * h + i] = s[:, i * CHUNK:(i + 1) * CHUNK]
    pos_score[...] = own_scores[0] + own_scores[1]
    near = [scores[14 + i] for i in range(4)]
    m = functools.reduce(jnp.maximum, near)
    top[...] = m
    total[...] = functools.reduce(jnp.add, [jnp.exp(s - m) for s in near])

    def process(slots):
        ks = [slot // 2 - (2 * g + 1) for slot in slots]

        @pl.when(slots[0] >= 0)
        def _():
            far = jnp.concatenate([buf[slot] for slot in slots], 0)
            s = lax.dot_general(
                buf[pl.ds(first, 4)].reshape(n, -1), far,
                (((1,), (1,)), ((), ())), preferred_element_type=F32) * scale
            for r in range(2):
                part = slice(r * BLOCK, (r + 1) * BLOCK)
                halves = [
                    jnp.where(alive(k, r), s[part, i * CHUNK:(i + 1) * CHUNK], NEG) for i, k in enumerate(ks)]
                for slot, value in zip(slots, halves):
                    scores[slot - (4 * g + 2), part, :] = value
                old = top[part, :]
                new = jnp.maximum(old, jnp.maximum(*halves))
                total[part, :] = total[part, :] * jnp.exp(old - new) + (
                    jnp.exp(halves[0] - new) + jnp.exp(halves[1] - new))
                top[part, :] = new

    def event(t, kind, i, sends):
        lists = plans[t][0]
        if kind == "T":
            when(z_send, lambda: got(rt.at[0], 2))
            slots = []
        elif kind == "Z":
            when(z_recv, lambda: got(rz.at[i], 2))
            slots = Z_IN[t][2 * i:2 * i + 2]
        else:
            slots = [{"X": X_IN, "Y": Y_IN}[kind][t][i]]
            sem = {"X": rx, "Y": ry}[kind].at[i if kind == "X" or i < LATE else 0]
            if i < LATE:
                when(z_recv if slots[0] < 16 else True, lambda: got(sem, 1))
            elif kind == "X":
                slots = [X_IN[t][i], Y_IN[t][i]]
                count = sum(s >= 16 for s in slots)
                if count == 2:
                    got(sem, 2)
                else:
                    when(z_recv, lambda: got(sem, 2))
                    if count:
                        when(~z_recv, lambda: got(sem, 1))
            else:
                slots = []
        for link, j in sends:
            link_send(t, lists, link, j)
        for s in slots:
            c_send(t, s)

    def c_wait(t, k, pair):
        sem = rc.at[pair_of(t, k, pair[0])]
        count = sum(s >= 16 for s in pair)
        if count == 2:
            got(sem, 2)
            return
        when(z_recv, lambda: got(sem, 2))
        if count:
            when(~z_recv, lambda: got(sem, 1))

    for u in range(STEPS):
        for t in range(2):
            @pl.when(yt == t)
            def _():
                for kind, i, sends in plans[t][2][u]:
                    event(t, kind, i, sends)
                for k in range(2):
                    now = pairs[t][k][u]
                    if now:
                        @pl.when(ct == k)
                        def _():
                            for pair in now:
                                c_wait(t, k, pair)
        for h in range(max(len(pairs[t][k][u]) for t in range(2) for k in range(2))):
            spots = [jnp.int32(-1), jnp.int32(-1)]
            for t in range(2):
                for k in range(2):
                    if h < len(pairs[t][k][u]):
                        here = (yt == t) & (ct == k)
                        spots = [jnp.where(here, slot_of(s), spot) for s, spot in zip(pairs[t][k][u][h], spots)]
            process(spots)

    eye = lax.broadcasted_iota(jnp.int32, (CHUNK, CHUNK), 0) == lax.broadcasted_iota(jnp.int32, (CHUNK, CHUNK), 1)

    def as_row(column):
        return jnp.sum(jnp.where(eye, jnp.broadcast_to(column, (CHUNK, CHUNK)), 0.0), axis=0, keepdims=True)

    lse_rows = []
    for i in range(n // CHUNK):
        part = slice(i * CHUNK, (i + 1) * CHUNK)
        m = jnp.max(top[part, :], axis=1, keepdims=True)
        t = jnp.sum(total[part, :] * jnp.exp(top[part, :] - m), axis=1, keepdims=True)
        lse_rows.append(as_row(m) + jnp.log(as_row(t)))
        lse_col[part, :] = m + jnp.log(t)
    for h in range(2):
        row = jnp.concatenate(lse_rows[2 * h:2 * h + 2], 1)
        lse_send[h] = row
        lse_far[2 * REACH + h] = row

    def lse_copy(offset):
        return copy(
            lse_send, lse_far.at[pl.ds(2 * (REACH - offset), 2)], ls.at[0], lr.at[0], me + offset)

    for offset in (-1, 1, -3, 3, -2, 2, -4, 4):
        when(exists(me + offset), lambda: lse_copy(offset).start())

    loss_ref[...] = jnp.concatenate([row - as_row(pos_score[i * CHUNK:(i + 1) * CHUNK, :]) for i, row in enumerate(lse_rows)], 1)[0]

    lows = []
    for r in range(2):
        low = jnp.int32(r)
        for k in range(r, 7 + r):
            low = low + jnp.where(alive(k, r), 0, 1)
        lows.append(low)

    def live(r, j):
        left = jnp.maximum(7 - lows[r], 0)
        return jnp.where(j < left, lows[r] + j, 9 + j - left)

    for h in range(2):
        s = jnp.concatenate([scores[14 + 2 * h + i] for i in range(2)], 1)
        w = jnp.exp(s - lse_col[...]) + jnp.exp(s - lse_far[2 * REACH + h])
        cell = lax.broadcasted_iota(jnp.int32, (n, BLOCK), 1) + h * BLOCK
        line = lax.broadcasted_iota(jnp.int32, (n, BLOCK), 0)
        w = w - (qcol_ref[...] == cell).astype(F32)
        w = w - (qrow_ref[0:1, h * BLOCK:(h + 1) * BLOCK] == line).astype(F32)
        weights[:, h * BLOCK:(h + 1) * BLOCK] = w.astype(jnp.bfloat16)

    width = e_hbm.shape[2]

    def own_product(t, carry):
        columns = pl.ds(pl.multiple_of(t * 256, 256), 256)
        grad_ref[:, columns] = jnp.dot(
            weights[:, :2 * BLOCK], buf[pl.ds(first, 4), :, columns].reshape(n, -1), preferred_element_type=F32)
        return carry

    lax.fori_loop(0, width // 256, own_product, 0)

    for r in range(2):
        part = pl.ds(r * BLOCK, BLOCK)
        for j in range(MOST - 1):
            for i in range(2):
                spot = slice((2 * j + i) * CHUNK, (2 * j + i + 1) * CHUNK)
                first_exp[part, spot] = jnp.exp(scores[2 * live(r, j) + i, part, :] - lse_col[part, :])

    partners = jnp.minimum(me, REACH) + jnp.minimum(devices - 1 - me, REACH)

    def lse_all(count):
        spot = lse_far.at[pl.ds(0, 2 * count)]
        return copy(spot, spot, ls.at[0], lr.at[0], cpeer)

    for count in range(REACH, 2 * REACH + 1):
        when(partners == count, lambda: lse_all(count).wait_recv())
    for r in range(2):
        part = pl.ds(r * BLOCK, BLOCK)
        for j in range(MOST - 1):
            far = lse_far[live(r, j) + 1]
            for i in range(2):
                spot = slice((2 * j + i) * CHUNK, (2 * j + i + 1) * CHUNK)
                w = first_exp[part, spot] + jnp.exp(
                    scores[2 * live(r, j) + i, part, :] - far[:, i * CHUNK:(i + 1) * CHUNK])
                weights[part, spot] = w.astype(jnp.bfloat16)

    for t in range(width // 256):
        columns = pl.ds(t * 256, 256)
        for r in range(2):
            part = pl.ds(r * BLOCK, BLOCK)
            near = jnp.concatenate(
                [buf[4 * g + 2 + 2 * live(r, j) + i, :, columns] for j in range(MOST - 1) for i in range(2)], 0)
            rest = jnp.dot(weights[part, :], near, preferred_element_type=F32)
            grad_ref[part, columns] = (grad_ref[part, columns] + rest) * scale

    for count in range(REACH, 2 * REACH + 1):
        when(partners == count, lambda: lse_all(count).wait_send())
    for t in range(2):
        conds = [link_cond(t, link, i) for link, items in plans[t][0].items() for i in range(len(items))] + ["R", "R"]
        arrivals = [s for steps in (X_IN[t], Y_IN[t], Z_IN[t]) for s in steps]
        for k in range(2):
            @pl.when((yt == t) & (ct == k))
            def _():
                relayed = [s for s in arrivals if k in c_need(t, s)]
                gone(sent.at[0], conds.count(True))
                when(z_send, lambda: gone(sent.at[1], conds.count("S")))
                when(z_recv, lambda: gone(sent.at[2], conds.count("R") + sum(s < 16 for s in relayed)))
                gone(sent.at[3], 8 + sum(s >= 16 for s in relayed))


def store(grad_ref, loss_ref, grad_out, loss_out, sem):
    parts = 4
    rows = grad_ref.shape[0] // parts
    copies = [pltpu.make_async_copy(loss_ref, loss_out, sem.at[parts])]
    for i in range(parts):
        spot = (pl.ds(i * rows, rows), slice(None))
        copies.append(pltpu.make_async_copy(grad_ref.at[spot], grad_out.at[spot], sem.at[i]))
    for todo in copies:
        todo.start()
    for todo in copies:
        todo.wait()


def solution(mesh):
    row_axis, col_axis = mesh.axis_names
    devices = mesh.shape[row_axis] * mesh.shape[col_axis]
    cols = mesh.shape[col_axis]

    def shards(embeddings, block_cluster, partner_shift):
        rows, width = embeddings.shape
        vmem = pl.BlockSpec(memory_space=pltpu.VMEM)
        hbm = pl.BlockSpec(memory_space=pl.ANY)
        grad, loss = pl.pallas_call(
            functools.partial(kernel, row_axis, col_axis, devices, cols, width ** (-0.5)),
            out_shape=(
                jax.ShapeDtypeStruct((rows, width), F32),
                jax.ShapeDtypeStruct((rows,), F32),
            ),
            in_specs=[hbm, hbm, hbm],
            out_specs=(vmem, vmem),
            scratch_shapes=[
                pltpu.VMEM((48, CHUNK, width), jnp.bfloat16),
                pltpu.VMEM((2 * HALF, width), jnp.bfloat16),
                pltpu.VMEM((32, rows, CHUNK), F32),
                pltpu.VMEM((rows, (MOST - 1) * BLOCK), F32),
                pltpu.VMEM((rows, (MOST - 1) * BLOCK), jnp.bfloat16),
                pltpu.VMEM((rows, CHUNK), F32),
                pltpu.VMEM((rows, CHUNK), F32),
                pltpu.VMEM((rows, 1), F32),
                pltpu.VMEM((2, 1, BLOCK), F32),
                pltpu.VMEM((2 * (2 * REACH + 1), 1, BLOCK), F32),
                pltpu.VMEM((rows, 1), F32),
                pltpu.VMEM((rows, 1), jnp.int32),
                pltpu.VMEM((1, rows), jnp.int32),
                pltpu.SMEM(block_cluster.shape, jnp.int32),
                pltpu.VMEM((1, rows), jnp.int32),
                pltpu.SemaphoreType.DMA((12,)),
                pltpu.SemaphoreType.DMA((LATE,)),
                pltpu.SemaphoreType.DMA((4,)),
                pltpu.SemaphoreType.DMA((1,)),
                pltpu.SemaphoreType.DMA((14,)),
                pltpu.SemaphoreType.DMA((4,)),
                pltpu.SemaphoreType.DMA((4,)),
                pltpu.SemaphoreType.DMA((1,)),
                pltpu.SemaphoreType.DMA((1,)),
                pltpu.SemaphoreType.DMA((3,)),
            ],
            compiler_params=pltpu.CompilerParams(
                collective_id=0, has_side_effects=True, vmem_limit_bytes=36 * 1024 * 1024
            ),
        )(*[pltpu.with_memory_space_constraint(a, pltpu.HBM) for a in (
            block_cluster, embeddings.reshape(rows // CHUNK, CHUNK, width), partner_shift.reshape(1, rows))])
        grad, loss = pl.pallas_call(
            store,
            out_shape=(jax.ShapeDtypeStruct(grad.shape, F32), jax.ShapeDtypeStruct(loss.shape, F32)),
            in_specs=[vmem, vmem],
            out_specs=(hbm, hbm),
            scratch_shapes=[pltpu.SemaphoreType.DMA((5,))],
            compiler_params=pltpu.CompilerParams(vmem_limit_bytes=36 * 1024 * 1024),
        )(grad, loss)
        return loss, grad

    in_specs = (P((row_axis, col_axis), None), P(), P((row_axis, col_axis)))
    out_specs = (P((row_axis, col_axis)), P((row_axis, col_axis), None))
    return jax.shard_map(shards, mesh=mesh, in_specs=in_specs, out_specs=out_specs, check_vma=False)
```

```python
import functools

import jax
import jax.numpy as jnp
from jax import lax
from jax.experimental import pallas as pl
from jax.experimental.pallas import tpu as pltpu
from jax.sharding import PartitionSpec as P

BLOCK = 256
MOST = 8
REACH = 4
CHUNK = 128
HALF = 64
NEG = -1e30
F32 = jnp.float32
MESH = pl.DeviceIdType.MESH

X_IN = (
    (40, 34, 41, 35, 36, 37, 38, 39, 32, 33, 10, 11),
    (38, 44, 39, 45, 43, 42, 14, 15, 33, 32, 37, 36),
)
Y_IN = (
    (20, 30, 21, 31, 22, 28, 23, 29, 12, 13, 14, 15),
    (27, 16, 26, 25, 24, 40, 41, 17, 18, 19, 34, 35),
)
Z_IN = (
    (8, 2, 9, 3, 4, 5, 6, 7),
    (6, 12, 7, 13, 11, 8, 10, 9),
)
BACK = ((17, 16), (21, 20))
OWN = (((16, 17, 18, 19), (24, 25, 26, 27)), ((20, 21, 22, 23), (28, 29, 30, 31)))
STEPS = 13


def pairs_of(t, k):
    low = 8 * k + 4 * t + 2
    ready = [[] for _ in range(STEPS)]
    for s in OWN[t][1 - k]:
        ready[0].append(s)
    for i in range(12):
        for s in (X_IN[t][i], Y_IN[t][i]):
            ready[i + 1].append(s)
    for i in range(8):
        ready[i // 2 * 2 + 4].append(Z_IN[t][i])
    pool, out = [], []
    for u in range(STEPS):
        pool += [s for s in ready[u] if low <= s < low + 32]
        now = []
        while len(pool) >= 2 and len(now) < 2:
            now.append((pool.pop(0), pool.pop(0)))
        out.append(now)
    assert not pool and sum(map(len, out)) == 14
    return out


def events_of(t):
    x_out = [("T", s - (14 if t == 0 else 10)) if s < 16 else ("S", 63 - s) for s in X_IN[1 - t]]
    y_out = [("S", s) for s in Y_IN[1 - t]]
    z_out = [("S", s + 32) for s in Z_IN[t]]
    lists = {"X": x_out, "Y": y_out, "Z": z_out}
    ahead = {"X": 0, "Y": 0, "Z": 0}
    have = {("S", s) for c in range(2) for s in OWN[t][c]}

    def ready():
        out = []
        for link, items in lists.items():
            while ahead[link] < len(items) and items[ahead[link]] in have:
                out.append((link, ahead[link]))
                ahead[link] += 1
        return out

    first = ready()
    steps = []
    for u in range(STEPS):
        now = []
        if u < 12:
            now += [("X", u, ("S", X_IN[t][u])), ("Y", u, ("S", Y_IN[t][u]))]
        if u == 1:
            now.append(("T", 0, ("T", 0), ("T", 1)))
        if u in (3, 5, 7, 9):
            now.append(("Z", (u - 3) // 2, *[("S", s) for s in Z_IN[t][u - 3:u - 1]]))
        done = []
        for kind, i, *items in now:
            have.update(items)
            done.append((kind, i, ready()))
        steps.append(done)
    assert all(ahead[link] == len(items) for link, items in lists.items())
    return lists, first, steps


def kernel(
    row_axis, col_axis, devices, cols, scale,
    cluster_hbm, e_hbm, shift_hbm,
    grad_ref, loss_ref,
    buf, thru, scores, first_exp, weights, top, total, lse_col, lse_send, lse_far, pos_score, qcol_ref, qrow_ref,
    cluster_ref, shift_ref,
    rx, ry, rz, rt, rc, ro, sent, ls, lr, own_sem,
):
    me = lax.axis_index(row_axis) * cols + lax.axis_index(col_axis)
    y = me % 2
    c = me // 2 % 2
    x = me // 4 % 2
    g = 2 * c + y
    yt = (x + y) % 2
    ct = (x + c) % 2
    xpeer = me + 4 - 8 * x
    ypeer = me + 1 - 2 * y
    cpeer = me + 2 - 4 * c
    zto = me + 8 - 16 * x
    zfrom = me - 8 + 16 * x
    z_send = (zto >= 0) & (zto < devices)
    z_recv = (zfrom >= 0) & (zfrom < devices)

    def at(device):
        return (device // cols, device % cols)

    def exists(device):
        return (device >= 0) & (device < devices)

    def when(cond, action):
        if cond is True:
            action()
        else:
            pl.when(cond)(action)

    def both(*conds):
        conds = [cond for cond in conds if cond is not True]
        return functools.reduce(lambda a, b: a & b, conds) if conds else True

    barrier = pltpu.get_barrier_semaphore()
    count = jnp.int32(0)
    for there, device in ((True, xpeer), (True, ypeer), (True, cpeer), (z_send, zto), (z_recv, zfrom)):
        when(there, lambda: pl.semaphore_signal(barrier, inc=1, device_id=at(device), device_id_type=MESH))
        count = count + (1 if there is True else there.astype(jnp.int32))
    pl.semaphore_wait(barrier, count)

    n = e_hbm.shape[0] * CHUNK
    first = 16 + 4 * g

    def slot_of(s):
        return s + x * (47 - 2 * s)

    def rows(slot, half):
        return buf.at[slot, pl.ds(pl.multiple_of(half * HALF, HALF), HALF), :]

    def copy(src, dst, send, receive, device):
        return pltpu.make_async_remote_copy(
            src_ref=src, dst_ref=dst, send_sem=send, recv_sem=receive,
            device_id=at(device), device_id_type=MESH,
        )

    def some(count):
        return buf.at[pl.ds(0, count), pl.ds(0, HALF), :]

    def got(sem, count):
        copy(some(count), some(count), sent.at[0], sem, cpeer).wait_recv()

    def gone(sem, count):
        if count:
            copy(some(count), some(count), sem, rt.at[0], cpeer).wait_send()

    def mine(s, half):
        return e_hbm.at[slot_of(s) - first, pl.ds(pl.multiple_of(half * HALF, HALF), HALF), :]

    def source(item, own):
        kind, s = item
        if kind == "T":
            return thru.at[pl.ds(s * HALF, HALF), :]
        return mine(s, c) if own else rows(slot_of(s), c)

    def link_cond(t, link, i):
        if link in "BZ":
            return "R" if link == "B" else "S"
        if link == "X":
            return "S" if X_IN[1 - t][i] < 16 else True
        return "R" if Y_IN[1 - t][i] < 16 else True

    def holds(cond):
        return {"S": z_send, "R": z_recv, True: True}[cond]

    def link_send(t, lists, link, i, own=False):
        cond = link_cond(t, link, i)
        sem = sent.at[{True: 0, "S": 1, "R": 2}[cond]]
        if link == "B":
            todo = copy(source(("S", BACK[t][i]), own), thru.at[pl.ds(i * HALF, HALF), :], sem, rt.at[0], zfrom)
        elif link == "X":
            s = X_IN[1 - t][i]
            todo = copy(source(lists[link][i], own), rows(s + (1 - x) * (47 - 2 * s), c), sem, rx.at[i], xpeer)
        elif link == "Y":
            todo = copy(source(lists[link][i], own), rows(slot_of(Y_IN[1 - t][i]), c), sem, ry.at[i], ypeer)
        else:
            todo = copy(source(lists[link][i], own), rows(slot_of(Z_IN[t][i]), c), sem, rz.at[i // 2], zto)
        when(holds(cond), lambda: todo.start())

    pairs = [[pairs_of(t, k) for k in range(2)] for t in range(2)]

    def pair_of(t, k, s):
        return [s in pair for now in pairs[t][k] for pair in now].index(True)

    def c_need(t, s):
        return [k for k in range(2) if 8 * (1 - k) + 4 * t + 2 <= s <= 8 * (1 - k) + 4 * t + 33]

    def c_send(t, s):
        for k in c_need(t, s):
            sem = sent.at[2 if s < 16 else 3]
            spot = rows(slot_of(s), c)
            when(both(ct == k, z_recv if s < 16 else True), lambda: copy(
                spot, spot, sem, rc.at[pair_of(t, 1 - k, s)], cpeer).start())

    plans = [events_of(t) for t in range(2)]

    own_copy = pltpu.make_async_copy(e_hbm, buf.at[pl.ds(first, 4)], own_sem.at[2])
    cluster_copy = pltpu.make_async_copy(cluster_hbm, cluster_ref, own_sem.at[0])
    shift_copy = pltpu.make_async_copy(shift_hbm, shift_ref, own_sem.at[1])
    for t in range(2):
        for k in range(2):
            @pl.when((yt == t) & (ct == k))
            def _():
                lists, first, _ = plans[t]
                opening = [(link, i) for link, i in first] + [("B", i) for i in range(2)]

                def slot_at(link, i):
                    return BACK[t][i] if link == "B" else lists[link][i][1]

                def send(link, i, own):
                    link_send(t, lists, link, i, own)

                queue = {link: [i for name, i in opening if name == link] for link in ("X", "Y", "B")}
                plan = {}
                for link, items in queue.items():
                    mine_, other = ([i for i in items if (slot_at(link, i) in OWN[t][k]) == flag] for flag in (True, False))
                    order = []
                    for spot in range(len(items)):
                        take = mine_ if (spot == 0 and mine_) or not other or (mine_ and mine_[0] < other[0]) else other
                        order.append(take.pop(0))
                    plan[link] = order
                leads = []
                for link in ("Y", "X", "B"):
                    while plan[link] and slot_at(link, plan[link][0]) in OWN[t][k]:
                        leads.append((link, plan[link].pop(0)))
                for link, i in leads[:2]:
                    send(link, i, True)
                uses = []
                for link in ("Y", "X", "B", "Y", "X", "B", "Y", "X", "B", "Y", "X", "B", "Y", "Y", "Y", "Y", "X", "X"):
                    if plan[link]:
                        uses.append((link, plan[link].pop(0)))
                assert not any(plan.values())
                order = []
                for s in [s for link, i in [*leads, *uses] for s in [slot_at(link, i)]] + list(OWN[t][k]):
                    if s in OWN[t][k] and s not in order:
                        order.append(s)
                for s in order:
                    copy(
                        mine(s, 1 - c), rows(slot_of(s), 1 - c), sent.at[3], ro.at[OWN[t][k].index(s)],
                        cpeer).start()
                for link, i in leads[2:]:
                    send(link, i, True)
                own_copy.start()
                cluster_copy.start()
                shift_copy.start()
                for s in order:
                    copy(
                        mine(s, c), rows(slot_of(s), c), sent.at[3], rc.at[pair_of(t, 1 - k, s)], cpeer).start()
                waited = set()
                for link, i in uses:
                    s = slot_at(link, i)
                    if s in OWN[t][k]:
                        send(link, i, True)
                        continue
                    if s not in waited:
                        waited.add(s)
                        got(ro.at[OWN[t][1 - k].index(s)], 1)
                    send(link, i, False)
                for s in OWN[t][1 - k]:
                    if s not in waited:
                        got(ro.at[OWN[t][1 - k].index(s)], 1)

    adj = 32 * x
    when(~z_recv, lambda: buf.__setitem__(
        pl.ds(adj, 16), jnp.zeros((16, *buf.shape[1:]), buf.dtype)))
    for offset in (-4, -3, -2, -1, 1, 2, 3, 4):
        when(~exists(me + offset), lambda: lse_far.__setitem__(
            pl.ds(2 * (offset + REACH), 2), jnp.zeros((2, *lse_far.shape[1:]), F32)))

    blocks = cluster_ref.shape[0]
    cluster_copy.wait()
    shift_copy.wait()

    def alive(k, r):
        there = 2 * me + k - 7
        near = jnp.maximum(jnp.minimum(there, blocks - 1), 0)
        same = cluster_ref[near] == cluster_ref[2 * me + r]
        return same & (there == near)

    place = lax.broadcasted_iota(jnp.int32, (1, n), 1)
    within = place % BLOCK
    goal = place - within + (within + shift_ref[...]) % BLOCK
    qrow_ref[...] = goal
    qcol_ref[...] = jnp.broadcast_to(goal.astype(F32), (128, n)).T[:, :1].astype(jnp.int32)

    own_copy.wait()
    half = lax.broadcasted_iota(jnp.int32, (n, BLOCK), 0)
    lane = lax.broadcasted_iota(jnp.int32, (n, BLOCK), 1)
    q = qcol_ref[...]
    own_scores = []
    for h in range(2):
        s = lax.dot_general(
            buf[pl.ds(first, 4)].reshape(n, -1), buf[pl.ds(first + 2 * h, 2)].reshape(BLOCK, -1), (((1,), (1,)), ((), ())),
            preferred_element_type=F32) * scale
        cell = lane + h * BLOCK
        hit = jnp.sum(jnp.where(q == cell, s, 0.0), axis=1, keepdims=True)
        own_scores.append(hit)
        ok = jnp.concatenate(
            [jnp.full((BLOCK, BLOCK), alive(7 + h, r).astype(jnp.int32), jnp.int32) for r in range(2)], 0) > 0
        s = jnp.where(ok & (half != cell), s, NEG)
        for i in range(2):
            scores[14 + 2 * h + i] = s[:, i * CHUNK:(i + 1) * CHUNK]
    pos_score[...] = own_scores[0] + own_scores[1]
    near = [scores[14 + i] for i in range(4)]
    m = functools.reduce(jnp.maximum, near)
    top[...] = m
    total[...] = functools.reduce(jnp.add, [jnp.exp(s - m) for s in near])

    def process(slots):
        ks = [slot // 2 - (2 * g + 1) for slot in slots]

        @pl.when(slots[0] >= 0)
        def _():
            far = jnp.concatenate([buf[slot] for slot in slots], 0)
            s = lax.dot_general(
                buf[pl.ds(first, 4)].reshape(n, -1), far,
                (((1,), (1,)), ((), ())), preferred_element_type=F32) * scale
            for r in range(2):
                part = slice(r * BLOCK, (r + 1) * BLOCK)
                halves = [
                    jnp.where(alive(k, r), s[part, i * CHUNK:(i + 1) * CHUNK], NEG) for i, k in enumerate(ks)]
                for slot, value in zip(slots, halves):
                    scores[slot - (4 * g + 2), part, :] = value
                old = top[part, :]
                new = jnp.maximum(old, jnp.maximum(*halves))
                total[part, :] = total[part, :] * jnp.exp(old - new) + (
                    jnp.exp(halves[0] - new) + jnp.exp(halves[1] - new))
                top[part, :] = new

    def event(t, kind, i, sends):
        lists = plans[t][0]
        if kind == "T":
            when(z_send, lambda: got(rt.at[0], 2))
            slots = []
        elif kind == "Z":
            when(z_recv, lambda: got(rz.at[i], 2))
            slots = Z_IN[t][2 * i:2 * i + 2]
        else:
            slots = [{"X": X_IN, "Y": Y_IN}[kind][t][i]]
            sem = {"X": rx, "Y": ry}[kind].at[i]
            when(z_recv if slots[0] < 16 else True, lambda: got(sem, 1))
        for link, j in sends:
            link_send(t, lists, link, j)
        for s in slots:
            c_send(t, s)

    def c_wait(t, k, pair):
        sem = rc.at[pair_of(t, k, pair[0])]
        count = sum(s >= 16 for s in pair)
        if count == 2:
            got(sem, 2)
            return
        when(z_recv, lambda: got(sem, 2))
        if count:
            when(~z_recv, lambda: got(sem, 1))

    for u in range(STEPS):
        for t in range(2):
            @pl.when(yt == t)
            def _():
                for kind, i, sends in plans[t][2][u]:
                    event(t, kind, i, sends)
                for k in range(2):
                    now = pairs[t][k][u]
                    if now:
                        @pl.when(ct == k)
                        def _():
                            for pair in now:
                                c_wait(t, k, pair)
        for h in range(max(len(pairs[t][k][u]) for t in range(2) for k in range(2))):
            spots = [jnp.int32(-1), jnp.int32(-1)]
            for t in range(2):
                for k in range(2):
                    if h < len(pairs[t][k][u]):
                        here = (yt == t) & (ct == k)
                        spots = [jnp.where(here, slot_of(s), spot) for s, spot in zip(pairs[t][k][u][h], spots)]
            process(spots)

    eye = lax.broadcasted_iota(jnp.int32, (CHUNK, CHUNK), 0) == lax.broadcasted_iota(jnp.int32, (CHUNK, CHUNK), 1)

    def as_row(column):
        return jnp.sum(jnp.where(eye, jnp.broadcast_to(column, (CHUNK, CHUNK)), 0.0), axis=0, keepdims=True)

    lse_rows = []
    for i in range(n // CHUNK):
        part = slice(i * CHUNK, (i + 1) * CHUNK)
        m = jnp.max(top[part, :], axis=1, keepdims=True)
        t = jnp.sum(total[part, :] * jnp.exp(top[part, :] - m), axis=1, keepdims=True)
        lse_rows.append(as_row(m) + jnp.log(as_row(t)))
        lse_col[part, :] = m + jnp.log(t)
    for h in range(2):
        row = jnp.concatenate(lse_rows[2 * h:2 * h + 2], 1)
        lse_send[h] = row
        lse_far[2 * REACH + h] = row

    def lse_copy(offset):
        return copy(
            lse_send, lse_far.at[pl.ds(2 * (REACH - offset), 2)], ls.at[0], lr.at[0], me + offset)

    for offset in (-1, 1, -3, 3, -2, 2, -4, 4):
        when(exists(me + offset), lambda: lse_copy(offset).start())

    loss_ref[...] = jnp.concatenate([row - as_row(pos_score[i * CHUNK:(i + 1) * CHUNK, :]) for i, row in enumerate(lse_rows)], 1)[0]

    lows = []
    for r in range(2):
        low = jnp.int32(r)
        for k in range(r, 7 + r):
            low = low + jnp.where(alive(k, r), 0, 1)
        lows.append(low)

    def live(r, j):
        left = jnp.maximum(7 - lows[r], 0)
        return jnp.where(j < left, lows[r] + j, 9 + j - left)

    for h in range(2):
        s = jnp.concatenate([scores[14 + 2 * h + i] for i in range(2)], 1)
        w = jnp.exp(s - lse_col[...]) + jnp.exp(s - lse_far[2 * REACH + h])
        cell = lax.broadcasted_iota(jnp.int32, (n, BLOCK), 1) + h * BLOCK
        line = lax.broadcasted_iota(jnp.int32, (n, BLOCK), 0)
        w = w - (qcol_ref[...] == cell).astype(F32)
        w = w - (qrow_ref[0:1, h * BLOCK:(h + 1) * BLOCK] == line).astype(F32)
        weights[:, h * BLOCK:(h + 1) * BLOCK] = w.astype(jnp.bfloat16)

    width = e_hbm.shape[2]

    def own_product(t, carry):
        columns = pl.ds(pl.multiple_of(t * 256, 256), 256)
        grad_ref[:, columns] = jnp.dot(
            weights[:, :2 * BLOCK], buf[pl.ds(first, 4), :, columns].reshape(n, -1), preferred_element_type=F32)
        return carry

    lax.fori_loop(0, width // 256, own_product, 0)

    for r in range(2):
        part = pl.ds(r * BLOCK, BLOCK)
        for j in range(MOST - 1):
            for i in range(2):
                spot = slice((2 * j + i) * CHUNK, (2 * j + i + 1) * CHUNK)
                first_exp[part, spot] = jnp.exp(scores[2 * live(r, j) + i, part, :] - lse_col[part, :])

    partners = jnp.minimum(me, REACH) + jnp.minimum(devices - 1 - me, REACH)

    def lse_all(count):
        spot = lse_far.at[pl.ds(0, 2 * count)]
        return copy(spot, spot, ls.at[0], lr.at[0], cpeer)

    for count in range(REACH, 2 * REACH + 1):
        when(partners == count, lambda: lse_all(count).wait_recv())
    for r in range(2):
        part = pl.ds(r * BLOCK, BLOCK)
        for j in range(MOST - 1):
            far = lse_far[live(r, j) + 1]
            for i in range(2):
                spot = slice((2 * j + i) * CHUNK, (2 * j + i + 1) * CHUNK)
                w = first_exp[part, spot] + jnp.exp(
                    scores[2 * live(r, j) + i, part, :] - far[:, i * CHUNK:(i + 1) * CHUNK])
                weights[part, spot] = w.astype(jnp.bfloat16)

    for t in range(width // 256):
        columns = pl.ds(t * 256, 256)
        for r in range(2):
            part = pl.ds(r * BLOCK, BLOCK)
            near = jnp.concatenate(
                [buf[4 * g + 2 + 2 * live(r, j) + i, :, columns] for j in range(MOST - 1) for i in range(2)], 0)
            rest = jnp.dot(weights[part, :], near, preferred_element_type=F32)
            grad_ref[part, columns] = (grad_ref[part, columns] + rest) * scale

    for count in range(REACH, 2 * REACH + 1):
        when(partners == count, lambda: lse_all(count).wait_send())
    for t in range(2):
        conds = [link_cond(t, link, i) for link, items in plans[t][0].items() for i in range(len(items))] + ["R", "R"]
        arrivals = [s for steps in (X_IN[t], Y_IN[t], Z_IN[t]) for s in steps]
        for k in range(2):
            @pl.when((yt == t) & (ct == k))
            def _():
                relayed = [s for s in arrivals if k in c_need(t, s)]
                gone(sent.at[0], conds.count(True))
                when(z_send, lambda: gone(sent.at[1], conds.count("S")))
                when(z_recv, lambda: gone(sent.at[2], conds.count("R") + sum(s < 16 for s in relayed)))
                gone(sent.at[3], 8 + sum(s >= 16 for s in relayed))


def store(grad_ref, loss_ref, grad_out, loss_out, sem):
    parts = 1
    rows = grad_ref.shape[0] // parts
    copies = [pltpu.make_async_copy(loss_ref, loss_out, sem.at[parts])]
    for i in range(parts):
        spot = (pl.ds(i * rows, rows), slice(None))
        copies.append(pltpu.make_async_copy(grad_ref.at[spot], grad_out.at[spot], sem.at[i]))
    for todo in copies:
        todo.start()
    for todo in copies:
        todo.wait()


def solution(mesh):
    row_axis, col_axis = mesh.axis_names
    devices = mesh.shape[row_axis] * mesh.shape[col_axis]
    cols = mesh.shape[col_axis]

    def shards(embeddings, block_cluster, partner_shift):
        rows, width = embeddings.shape
        vmem = pl.BlockSpec(memory_space=pltpu.VMEM)
        hbm = pl.BlockSpec(memory_space=pl.ANY)
        grad, loss = pl.pallas_call(
            functools.partial(kernel, row_axis, col_axis, devices, cols, width ** (-0.5)),
            out_shape=(
                jax.ShapeDtypeStruct((rows, width), F32),
                jax.ShapeDtypeStruct((rows,), F32),
            ),
            in_specs=[hbm, hbm, hbm],
            out_specs=(vmem, vmem),
            scratch_shapes=[
                pltpu.VMEM((48, CHUNK, width), jnp.bfloat16),
                pltpu.VMEM((2 * HALF, width), jnp.bfloat16),
                pltpu.VMEM((32, rows, CHUNK), F32),
                pltpu.VMEM((rows, (MOST - 1) * BLOCK), F32),
                pltpu.VMEM((rows, (MOST - 1) * BLOCK), jnp.bfloat16),
                pltpu.VMEM((rows, CHUNK), F32),
                pltpu.VMEM((rows, CHUNK), F32),
                pltpu.VMEM((rows, 1), F32),
                pltpu.VMEM((2, 1, BLOCK), F32),
                pltpu.VMEM((2 * (2 * REACH + 1), 1, BLOCK), F32),
                pltpu.VMEM((rows, 1), F32),
                pltpu.VMEM((rows, 1), jnp.int32),
                pltpu.VMEM((1, rows), jnp.int32),
                pltpu.SMEM(block_cluster.shape, jnp.int32),
                pltpu.VMEM((1, rows), jnp.int32),
                pltpu.SemaphoreType.DMA((12,)),
                pltpu.SemaphoreType.DMA((12,)),
                pltpu.SemaphoreType.DMA((4,)),
                pltpu.SemaphoreType.DMA((1,)),
                pltpu.SemaphoreType.DMA((14,)),
                pltpu.SemaphoreType.DMA((4,)),
                pltpu.SemaphoreType.DMA((4,)),
                pltpu.SemaphoreType.DMA((1,)),
                pltpu.SemaphoreType.DMA((1,)),
                pltpu.SemaphoreType.DMA((3,)),
            ],
            compiler_params=pltpu.CompilerParams(
                collective_id=0, has_side_effects=True, vmem_limit_bytes=36 * 1024 * 1024
            ),
        )(*[pltpu.with_memory_space_constraint(a, pltpu.HBM) for a in (
            block_cluster, embeddings.reshape(rows // CHUNK, CHUNK, width), partner_shift.reshape(1, rows))])
        grad, loss = pl.pallas_call(
            store,
            out_shape=(jax.ShapeDtypeStruct(grad.shape, F32), jax.ShapeDtypeStruct(loss.shape, F32)),
            in_specs=[vmem, vmem],
            out_specs=(hbm, hbm),
            scratch_shapes=[pltpu.SemaphoreType.DMA((2,))],
            compiler_params=pltpu.CompilerParams(vmem_limit_bytes=36 * 1024 * 1024),
        )(grad, loss)
        return loss, grad

    in_specs = (P((row_axis, col_axis), None), P(), P((row_axis, col_axis)))
    out_specs = (P((row_axis, col_axis)), P((row_axis, col_axis), None))
    return jax.shard_map(shards, mesh=mesh, in_specs=in_specs, out_specs=out_specs, check_vma=False)
```
